1024 devices in a mesh: fsdp: 128 (over z_lo, y, core), tensor: 8 (over x, z_hi).
Axes of the slice: x: 4, y: 4, z: 32 (z_hi: 2, z_lo: 16; z = z_hi * 16 + z_lo), core: 2. Of those that a mesh axis runs over, the one named last changes fastest.
Arguments:
- new_hidden: bfloat16 [2048, 2, 8192], P('fsdp'), may hold values from -6 to 6
- new_queries: bfloat16 [2048, 2, 8192], P('fsdp', None, 'tensor'), may hold values from -540 to 540
- paged_cache: bfloat16 [4096, 64, 2048], P('fsdp', None, 'tensor'), may hold values from -6 to 6
- block_table: int32 [2048, 8], P('fsdp'), may hold values from 0 to 31
- lengths: int32 [2048], P('fsdp'), may hold values from 1 to 512
- destination: int32 [2048], P('fsdp'), may hold values from -1 to 127, as said below
- train_hidden: bfloat16 [8192, 8192], P('fsdp'), may hold values from -6 to 6
- train_queries: bfloat16 [8192, 8192], P('fsdp', 'tensor'), may hold values from -540 to 540
- documents: int32 [128, 64], P('fsdp'), may hold values from 0 to 3, never falling along the last dimension, each value on 1 to 32 neighbouring positions
- project_weight: bfloat16 [8192, 2048], P('fsdp', 'tensor'), may hold values from -0.0625 to 0.0625
- project_bias: float32 [2048], P('tensor'), may hold values from -3 to 3
Outputs:
- decoded: bfloat16 [2048, 2, 8192], P('fsdp', None, 'tensor')
- train_attention: bfloat16 [8192, 8192], P('fsdp', 'tensor')
- handover: bfloat16 [16384, 2, 2048], P('fsdp', None, 'tensor')
The draws below stay inside these ranges and needn't reach their ends.
Inputs may be any that keep to these rules, and one draw needn't show every extreme that they name: `destination`: the rows of one fsdp index name each training shard at most once.
All inputs are finite; a program needn't handle non-finite values.
Results may differ from the reference program's by a relative error of at most 0.0095.
Values may be sent and summed in bfloat16 or wider, within the bound.
A program may use at most 64 MiB of HBM per device.

```python
import math
import jax
import jax.numpy as jnp
import numpy as np
from jax import lax

D = 8192
HEADS = 64
KV_HEADS = 8
HEAD_DIM = 128
ROWS_DEV = 16
TRAIN_DEV = 64
PAGE = 64
MAX_PAGES = 8
POOL_DEV = 32
ROWS = 2048
TRAIN = 8192
POOL = 4096
N_FSDP = 128


def draw_destination(key, part):
    groups = ROWS // ROWS_DEV
    spread_count = max(ROWS_DEV, groups)

    def per_group(group_key):
        first_key, second_key = jax.random.split(group_key)
        order = jax.random.permutation(first_key, spread_count)[:ROWS_DEV]
        finish = jax.random.randint(second_key, (ROWS_DEV,), 0, 4)
        return jnp.where((order < groups) & (finish > 0), order, -1).astype(jnp.int32)
    return jax.vmap(per_group)(jax.random.split(key, groups)).reshape(ROWS)


def draw_new_queries(key, part):
    values = jnp.clip(jax.random.normal(key, (ROWS, 2, HEADS * HEAD_DIM), jnp.float32), -6.0, 6.0)
    return values.astype(jnp.bfloat16)


def draw_train_queries(key, part):
    values = jnp.clip(jax.random.normal(key, (TRAIN, HEADS * HEAD_DIM), jnp.float32), -6.0, 6.0)
    return values.astype(jnp.bfloat16)


def set_ends(array, own_key, low, high):
    longest = array.shape.index(max(array.shape))
    spots = []
    for shift in (0, 1):
        where = [jax.random.randint(jax.random.fold_in(own_key, axis), (), 0, length) for axis, length in enumerate(array.shape)]
        where[longest] = (where[longest] + shift) % array.shape[longest]
        spots.append(tuple(where))
    return array.at[spots[0]].set(low).at[spots[1]].set(high)


def block_scale(stream_key, shape, cuts, smallest, top_value):
    gain = 1.0
    for dim, shards_of in cuts:
        steps = jax.random.uniform(jax.random.fold_in(jax.random.fold_in(stream_key, 6), dim), (shards_of,), jnp.float32, smallest / len(cuts), top_value / len(cuts))
        gain = gain * jnp.repeat(jnp.exp(steps), shape[dim] // shards_of).reshape((-1,) + (1,) * (len(shape) - 1 - dim))
    return gain


def split_up(count, total, limit, skew):
    loads = [(1 << 20) // math.isqrt(rank ** skew) + 1 for rank in range(2, count + 1)]
    surplus, given = total - limit - (count - 1), [1] * (count - 1)
    while surplus > 0:
        free = [i for i in range(count - 1) if given[i] < limit]
        pool, budget = sum([loads[i] for i in free]), surplus
        for i in free:
            extra = min(limit - given[i], max(1, budget * loads[i] // pool), surplus)
            given[i] = given[i] + extra
            surplus = surplus - extra
    return np.array([limit] + given)


def uneven_parts(own_key, amount, total, bound, lean):
    if amount == 2:
        one = jax.random.randint(own_key, (), max(1, total - bound), min(bound, total - 1) + 1)
        return jnp.stack([one, total - one])
    tallies = jnp.asarray(split_up(amount, total, bound, lean), jnp.int32)
    couples = (amount - 1) // 2
    giver, receiver = tallies[1:1 + 2 * couples:2], tallies[2:2 + 2 * couples:2]
    margin = jnp.minimum(giver - 1, bound - receiver)
    passed = jax.random.randint(jax.random.fold_in(own_key, 1), (couples,), 0, 1 << 20) % (margin + 1)
    tallies = tallies.at[1:1 + 2 * couples:2].set(giver - passed).at[2:2 + 2 * couples:2].set(receiver + passed)
    return tallies[jax.random.permutation(jax.random.fold_in(own_key, 2), amount)]


def noise(key, shape, scale, limit, cuts=(), held_as=jnp.bfloat16):
    values = jax.random.normal(key, shape, jnp.float32) * scale
    if len(cuts) > 0:
        values = block_scale(key, shape, cuts, -0.22, 0.18) * values
    return jnp.clip(values, min=-limit, max=limit).astype(held_as)


def setup_inputs(seed: int = 0) -> dict:
    seeds = jax.random.split(jax.random.key(seed), 12)
    new_hidden = noise(seeds[0], (ROWS, 2, D), 1.0, 6.0, ((0, 128),))
    new_queries = draw_new_queries(jax.random.fold_in(seeds[11], 71), 0)
    paged_cache = noise(seeds[2], (POOL, PAGE, 2 * KV_HEADS * HEAD_DIM), 1.0, 6.0, ((0, 128), (2, 8)))
    block_table = set_ends(jax.random.randint(seeds[3], (ROWS, MAX_PAGES), 0, POOL_DEV), jax.random.fold_in(seeds[3], 1), 0, POOL_DEV - 1).astype(jnp.int32)
    lengths = set_ends(jax.random.randint(seeds[4], (ROWS,), 1, PAGE * MAX_PAGES + 1), jax.random.fold_in(seeds[4], 1), 1, PAGE * MAX_PAGES).astype(jnp.int32)
    destination = draw_destination(jax.random.fold_in(seeds[11], 71), 0)
    train_hidden = noise(seeds[6], (TRAIN, D), 1.0, 6.0, ((0, 128),))
    train_queries = draw_train_queries(jax.random.fold_in(seeds[11], 71), 0)
    documents = jax.vmap(lambda own: jnp.searchsorted(jnp.cumsum(uneven_parts(own, 4, TRAIN_DEV, TRAIN_DEV // 2, 0)), jnp.arange(TRAIN_DEV), side="right"))(jax.random.split(seeds[8], N_FSDP)).reshape((N_FSDP, TRAIN_DEV)).astype(jnp.int32)
    project_weight = noise(seeds[9], (D, 2 * KV_HEADS * HEAD_DIM), D ** -0.5, 0.0625, ((0, 128), (1, 8)))
    project_bias = noise(seeds[10], (2 * KV_HEADS * HEAD_DIM,), 0.5, 3.0, ((0, 8),), jnp.float32)
    return dict(new_hidden=new_hidden, new_queries=new_queries, paged_cache=paged_cache, block_table=block_table, lengths=lengths, destination=destination, train_hidden=train_hidden, train_queries=train_queries, documents=documents, project_weight=project_weight, project_bias=project_bias)


masked_value = -1.0e30


def decode_group(operands):
    queries, tables, spans, fresh_rows, cache_pool = operands
    context = PAGE * MAX_PAGES
    group_size = HEADS // KV_HEADS
    scaling = HEAD_DIM ** -0.5
    cached = cache_pool[tables].reshape(ROWS_DEV, context, KV_HEADS, 2, HEAD_DIM).astype(jnp.float32)
    fresh_wide = fresh_rows.astype(jnp.float32)
    heads_q = queries.reshape(ROWS_DEV, 2, KV_HEADS, group_size, HEAD_DIM).astype(jnp.float32)
    old_scores = jnp.einsum('btkgd,bckd->btkgc', heads_q, cached[:, :, :, 0, :]) * scaling
    places = jnp.arange(context, dtype=jnp.int32)
    allowed_old = places[None, :] < spans[:, None]
    old_scores = jnp.where(allowed_old[:, None, None, None, :], old_scores, masked_value)
    new_scores = jnp.einsum('btkgd,bskd->btkgs', heads_q, fresh_wide[:, :, :, 0, :]) * scaling
    order = jnp.arange(2, dtype=jnp.int32)
    allowed_new = order[None, :] <= order[:, None]
    new_scores = jnp.where(allowed_new[None, :, None, None, :], new_scores, masked_value)
    highest = jnp.maximum(jnp.max(old_scores, -1, keepdims=True), jnp.max(new_scores, -1, keepdims=True))
    old_exp = jnp.exp(old_scores - highest)
    new_exp = jnp.exp(new_scores - highest)
    totals = jnp.sum(old_exp, -1, keepdims=True) + jnp.sum(new_exp, -1, keepdims=True)
    old_weights = lax.optimization_barrier((old_exp / totals).astype(jnp.bfloat16)).astype(jnp.float32)
    new_weights = lax.optimization_barrier((new_exp / totals).astype(jnp.bfloat16)).astype(jnp.float32)
    result = jnp.einsum('btkgc,bckd->btkgd', old_weights, cached[:, :, :, 1, :])
    result = result + jnp.einsum('btkgs,bskd->btkgd', new_weights, fresh_wide[:, :, :, 1, :])
    return result.astype(jnp.bfloat16).reshape(ROWS_DEV, 2, HEADS * HEAD_DIM)


def train_group(operands):
    queries, keyvals, doc_row = operands
    group_size = HEADS // KV_HEADS
    scaling = HEAD_DIM ** -0.5
    heads_q = queries.reshape(TRAIN_DEV, KV_HEADS, group_size, HEAD_DIM).astype(jnp.float32)
    wide_kv = keyvals.astype(jnp.float32)
    scores = jnp.einsum('tkgd,skd->kgts', heads_q, wide_kv[:, :, 0, :]) * scaling
    places = jnp.arange(TRAIN_DEV, dtype=jnp.int32)
    allowed = (places[None, :] <= places[:, None]) & (doc_row[None, :] == doc_row[:, None])
    scores = jnp.where(allowed[None, None, :, :], scores, masked_value)
    highest = jnp.max(scores, -1, keepdims=True)
    expo = jnp.exp(scores - highest)
    weights = expo / jnp.sum(expo, -1, keepdims=True)
    weights = lax.optimization_barrier(weights.astype(jnp.bfloat16)).astype(jnp.float32)
    result = jnp.einsum('kgts,skd->tkgd', weights, wide_kv[:, :, 1, :])
    return result.astype(jnp.bfloat16).reshape(TRAIN_DEV, HEADS * HEAD_DIM)


def reference(new_hidden, new_queries, paged_cache, block_table, lengths, destination, train_hidden, train_queries, documents, project_weight, project_bias):
    groups = N_FSDP
    columns = 2 * KV_HEADS * HEAD_DIM
    fresh = jnp.dot(new_hidden.reshape(ROWS * 2, D), project_weight, preferred_element_type=jnp.float32) + project_bias
    fresh = fresh.astype(jnp.bfloat16).reshape(ROWS, 2, KV_HEADS, 2, HEAD_DIM)
    train_kv = jnp.dot(train_hidden, project_weight, preferred_element_type=jnp.float32) + project_bias
    train_kv = train_kv.astype(jnp.bfloat16).reshape(TRAIN, KV_HEADS, 2, HEAD_DIM)
    slot_index = jnp.where(destination >= 0, destination * groups + jnp.arange(ROWS, dtype=jnp.int32) // ROWS_DEV, groups * groups).astype(jnp.int32)
    handover = jnp.zeros((groups * groups + 1, 2, columns), jnp.bfloat16).at[slot_index].set(fresh.reshape(ROWS, 2, columns))[:groups * groups]
    decoded = lax.map(decode_group, (new_queries.reshape(groups, ROWS_DEV, 2, HEADS * HEAD_DIM), block_table.reshape(groups, ROWS_DEV, MAX_PAGES), lengths.reshape(groups, ROWS_DEV), fresh.reshape(groups, ROWS_DEV, 2, KV_HEADS, 2, HEAD_DIM), paged_cache.reshape(groups, POOL_DEV, PAGE, columns)))
    decoded = decoded.reshape(ROWS, 2, HEADS * HEAD_DIM)
    train_attention = lax.map(train_group, (train_queries.reshape(groups, TRAIN_DEV, HEADS * HEAD_DIM), train_kv.reshape(groups, TRAIN_DEV, KV_HEADS, 2, HEAD_DIM), documents))
    train_attention = train_attention.reshape(TRAIN, HEADS * HEAD_DIM)
    return decoded, train_attention, handover
```

```python
import jax
import jax.numpy as jnp
from jax import lax
from jax.experimental import pallas as pl
from jax.experimental.pallas import tpu as pltpu
from jax.sharding import PartitionSpec as P

HEADS = 64
KV_HEADS = 8
HEAD_DIM = 128
GROUP = HEADS // KV_HEADS
MESH = pl.DeviceIdType.MESH
SCALE = HEAD_DIM ** (-0.5)
MASKED = -1e30

RUNS = 4
PLACES = 4
YS = 4
CORES = 2
ROWS_DEV = 16
TRAIN_DEV = 64
BLOCK = 64
WIDTH = 8192
COLS = 256
PAGE = 64
MAX_PAGES = 8
CONTEXT = PAGE * MAX_PAGES
NEW = ROWS_DEV * 2


def dot_nt(a, b):
    return lax.dot_general(a, b, (((1,), (1,)), ((), ())), preferred_element_type=jnp.float32)


def kernel(
    table_ref,
    length_ref,
    destination_ref,
    documents_ref,
    bias_ref,
    queries_ref,
    train_queries_ref,
    new_hidden_hbm,
    train_hidden_hbm,
    cache_hbm,
    weight_hbm,
    decoded_ref,
    train_out_ref,
    handover_ref,
    wbuf,
    hbuf,
    pool,
    mbuf,
    fbuf,
    acc,
    kvbuf,
    scores,
    hstage,
    hrecv,
    local_sem,
    w_chain_send,
    w_chain_recv,
    w_group_send,
    w_group_recv,
    m_chain_send,
    m_chain_recv,
    m_group_send,
    m_group_recv,
    f_chain_send,
    f_chain_recv,
    f_group_send,
    f_group_recv,
    y_send,
    y_relay_send,
    y_recv,
    p_send,
    p_recv,
    h_send,
    h_recv,
):
    me = lax.axis_index("fsdp")
    core = me % CORES
    y = (me // CORES) % YS
    z = me // (CORES * YS)
    place = z % PLACES
    run = z // PLACES
    y_before = (y + YS - 1) % YS
    y_after = (y + 1) % YS
    y_across = (y + 2) % YS
    other = 1 - core
    octet = y * CORES + core

    def device(zz, yy, cc):
        return (zz * YS + yy) * CORES + cc

    def remote(src, dst, ssem, rsem, target):
        return pltpu.make_async_remote_copy(
            src_ref=src,
            dst_ref=dst,
            send_sem=ssem,
            recv_sem=rsem,
            device_id={"fsdp": target},
            device_id_type=MESH,
        )

    def when(cond, do):
        if cond is True:
            do()
        else:
            pl.when(cond)(do)

    def both(a, b):
        if a is True:
            return b
        if b is True:
            return a
        return jnp.logical_and(a, b)

    pending = []

    def send(cond, make):
        when(cond, lambda: make().start())
        pending.append((cond, make))

    def settle():
        for cond, make in pending:
            when(cond, lambda make=make: make().wait_send())
        pending.clear()

    own_w = wbuf.at[y, run, place, core]
    w_copy = pltpu.make_async_copy(weight_hbm, own_w, local_sem.at[0])
    pool_copy = pltpu.make_async_copy(cache_hbm, pool, local_sem.at[1])
    new_copy = pltpu.make_async_copy(new_hidden_hbm, hbuf.at[pl.ds(0, NEW)], local_sem.at[2])
    train_copy = pltpu.make_async_copy(
        train_hidden_hbm, hbuf.at[pl.ds(NEW, TRAIN_DEV)], local_sem.at[3]
    )
    w_copy.start()
    pool_copy.start()
    new_copy.start()
    train_copy.start()

    lane = lax.broadcasted_iota(jnp.int32, (1, 128), 1)
    wanted = jnp.zeros((1, 128), jnp.float32)
    for r in range(ROWS_DEV):
        value = (destination_ref[r] + 1).astype(jnp.float32)
        hit = (lane // NEW == place) & ((lane % NEW) // 2 == r)
        wanted = jnp.where(hit, value, wanted)
    mbuf[run, place] = wanted

    barrier = pltpu.get_barrier_semaphore()
    for step in range(1, YS * CORES):
        pl.semaphore_signal(
            barrier,
            inc=1,
            device_id={"fsdp": z * (YS * CORES) + (octet + step) % (YS * CORES)},
            device_id_type=MESH,
        )
    expected = jnp.int32(YS * CORES - 1)
    for cond, zz in (
        (run > 0, z - PLACES),
        (run < RUNS - 1, z + PLACES),
        (place > 0, z - 1),
        (place < PLACES - 1, z + 1),
    ):

        @pl.when(cond)
        def _(zz=zz):
            pl.semaphore_signal(
                barrier, inc=1, device_id={"fsdp": device(zz, y, core)}, device_id_type=MESH
            )

        expected = expected + cond.astype(jnp.int32)
    pl.semaphore_wait(barrier, expected)

    class Along:
        def __init__(self, parts):
            self.parts = parts

        def chain_send(self, cond, side, rr, first=False):
            for block, source, cs, cr, _, _ in self.parts:
                src = source if (first and source is not None) else block(rr, place)
                send(
                    cond,
                    lambda src=src, block=block, cs=cs, cr=cr: remote(
                        src,
                        block(rr, place),
                        cs.at[(side + 1) // 2, rr],
                        cr.at[rr],
                        device(z + PLACES * side, y, core),
                    ),
                )

        def chain_wait(self, rr):
            for block, _, cs, cr, _, _ in self.parts:
                remote(
                    block(rr, place), block(rr, place), cs.at[0, rr], cr.at[rr], device(z, y, other)
                ).wait_recv()

        def group_send(self, cond, side, rr, pp, first=False):
            for block, source, _, _, gs, gr in self.parts:
                src = source if (first and source is not None) else block(rr, pp)
                send(
                    cond,
                    lambda src=src, block=block, gs=gs, gr=gr: remote(
                        src,
                        block(rr, pp),
                        gs.at[(side + 1) // 2, rr, pp],
                        gr.at[rr, pp],
                        device(z + side, y, core),
                    ),
                )

        def group_wait(self, rr, pp):
            for block, _, _, _, gs, gr in self.parts:
                remote(
                    block(rr, pp),
                    block(rr, pp),
                    gs.at[0, rr, pp],
                    gr.at[rr, pp],
                    device(z, y, other),
                ).wait_recv()

        def start(self):
            self.chain_send(run < RUNS - 1, 1, run, first=True)
            self.chain_send(run > 0, -1, run, first=True)

        def chain(self, d):
            low, high = run - d, run + d
            when(low >= 0, lambda: self.chain_wait(low))
            self.chain_send(both(low >= 0, run < RUNS - 1), 1, low)
            when(high < RUNS, lambda: self.chain_wait(high))
            self.chain_send(both(high < RUNS, run > 0), -1, high)

        def spread(self, d):
            for cond, rr in quads(d):
                self.group_send(both(cond, place < PLACES - 1), 1, rr, place, first=d == 0)
                self.group_send(both(cond, place > 0), -1, rr, place, first=d == 0)

        def step(self, d, k):
            low, high = place - k, place + k
            for cond, rr in quads(d):
                when(both(cond, low >= 0), lambda rr=rr: self.group_wait(rr, low))
                self.group_send(
                    both(cond, both(low >= 0, place < PLACES - 1)), 1, rr, low
                )
                when(both(cond, high < PLACES), lambda rr=rr: self.group_wait(rr, high))
                self.group_send(both(cond, both(high < PLACES, place > 0)), -1, rr, high)

    def quads(d):
        if d == 0:
            return [(True, run)]
        return [(run - d >= 0, run - d), (run + d < RUNS, run + d)]

    weights = Along(
        [
            (
                lambda rr, pp: wbuf.at[y, rr, pp, core],
                weight_hbm,
                w_chain_send,
                w_chain_recv,
                w_group_send,
                w_group_recv,
            ),
            (
                lambda rr, pp: mbuf.at[rr, pp],
                None,
                m_chain_send,
                m_chain_recv,
                m_group_send,
                m_group_recv,
            ),
        ]
    )

    def quad(yy, rr):
        return wbuf.at[yy, rr, :, core]

    def pass_over(cond, yy, rr):
        send(
            cond,
            lambda: remote(
                quad(yy, rr),
                quad(yy, rr),
                p_send.at[yy, rr],
                p_recv.at[yy, rr],
                device(z, y, other),
            ),
        )

    def y_out(d):
        for cond, rr in quads(d):
            for side, yy in ((0, y_before), (1, y_after)):
                send(
                    cond,
                    lambda rr=rr, side=side, yy=yy: remote(
                        quad(y, rr),
                        quad(y, rr),
                        y_send.at[side, rr],
                        y_recv.at[y, rr],
                        device(z, yy, core),
                    ),
                )
            pass_over(cond, y, rr)

    def y_wait(yy, rr):
        remote(
            quad(yy, rr), quad(yy, rr), y_send.at[0, rr], y_recv.at[yy, rr], device(z, y, other)
        ).wait_recv()

    def y_in(d):
        source = jnp.where(core == 0, y_before, y_after)
        target = jnp.where(core == 0, y_after, y_before)
        for cond, rr in quads(d):
            when(cond, lambda rr=rr: y_wait(source, rr))
            send(
                cond,
                lambda rr=rr: remote(
                    quad(source, rr),
                    quad(source, rr),
                    y_relay_send.at[rr],
                    y_recv.at[source, rr],
                    device(z, target, core),
                ),
            )
            pass_over(cond, source, rr)
            when(cond, lambda rr=rr: y_wait(target, rr))
            pass_over(cond, target, rr)

    def y_last(d):
        for cond, rr in quads(d):
            when(cond, lambda rr=rr: y_wait(y_across, rr))
            pass_over(cond, y_across, rr)

    def partner_wait(yy, rr):
        landed = wbuf.at[yy, rr, :, other]
        remote(
            landed, landed, p_send.at[yy, rr], p_recv.at[yy, rr], device(z, y, other)
        ).wait_recv()

    def multiply(yy, rr):
        partner_wait(yy, rr)
        parts = []
        for pp in range(PLACES):
            start = ((rr * PLACES + pp) * YS + yy) * (CORES * BLOCK)
            parts.append(hbuf[:, pl.ds(pl.multiple_of(start, 128), CORES * BLOCK)])
        left = jnp.concatenate(parts, axis=1)
        right = wbuf[yy, rr].reshape(PLACES * CORES * BLOCK, COLS)
        acc[...] += jnp.dot(left, right, preferred_element_type=jnp.float32)

    def multiply_near(d):
        for cond, rr in quads(d):

            def do(rr=rr):
                for yy in (y, y_before, y_after):
                    multiply(yy, rr)

            when(cond, do)

    def multiply_far(d):
        for cond, rr in quads(d):
            when(cond, lambda rr=rr: multiply(y_across, rr))

    position = lax.broadcasted_iota(jnp.int32, (1, CONTEXT), 1)

    def old_scores(rows):
        for r in rows:
            keys = jnp.concatenate(
                [pool[table_ref[r, p], :, 0:HEAD_DIM] for p in range(MAX_PAGES)], axis=0
            )
            values = dot_nt(queries_ref[r], keys) * SCALE
            scores[r] = jnp.where(position < length_ref[r], values, MASKED)

    acc[...] = jnp.zeros_like(acc)
    weights.start()
    weights.spread(0)
    pool_copy.wait()
    old_scores(range(0, 2))
    weights.step(0, 1)
    old_scores(range(2, 4))
    weights.step(0, 2)
    weights.chain(1)
    weights.spread(1)
    weights.step(0, 3)
    w_copy.wait()
    y_out(0)
    old_scores(range(4, 6))
    weights.step(1, 1)
    old_scores(range(6, 8))
    weights.step(1, 2)
    weights.chain(2)
    weights.spread(2)
    weights.step(1, 3)
    y_out(1)
    y_in(0)
    old_scores(range(8, 10))
    weights.step(2, 1)
    old_scores(range(10, 12))
    weights.step(2, 2)
    weights.chain(3)
    weights.spread(3)
    weights.step(2, 3)
    y_out(2)
    y_in(1)
    y_last(0)
    old_scores(range(12, 14))
    weights.step(3, 1)
    old_scores(range(14, 16))
    weights.step(3, 2)
    weights.step(3, 3)
    y_out(3)
    new_copy.wait()
    train_copy.wait()
    multiply_near(0)
    y_in(2)
    y_last(1)
    multiply_far(0)
    multiply_near(1)
    y_in(3)
    y_last(2)
    multiply_far(1)
    multiply_near(2)
    y_last(3)
    multiply_far(2)
    multiply_near(3)
    multiply_far(3)

    fresh = (acc[...] + bias_ref[...]).astype(jnp.bfloat16)
    fbuf[run, place] = fresh[0:NEW]
    kvbuf[...] = fresh

    rows_z = Along(
        [
            (
                lambda rr, pp: fbuf.at[rr, pp],
                None,
                f_chain_send,
                f_chain_recv,
                f_group_send,
                f_group_recv,
            )
        ]
    )

    new_column = lax.broadcasted_iota(jnp.int32, (CORES * GROUP, NEW), 1)
    new_token = lax.broadcasted_iota(jnp.int32, (CORES * GROUP, NEW), 0) // GROUP

    def decode(rows):
        for r in rows:
            values = jnp.concatenate(
                [pool[table_ref[r, p], :, HEAD_DIM : 2 * HEAD_DIM] for p in range(MAX_PAGES)],
                axis=0,
            )
            old = scores[r]
            new = dot_nt(queries_ref[r], kvbuf[0:NEW, 0:HEAD_DIM]) * SCALE
            allowed = (new_column // 2 == r) & (new_column % 2 <= new_token)
            new = jnp.where(allowed, new, MASKED)
            highest = jnp.maximum(
                jnp.max(old, axis=1, keepdims=True), jnp.max(new, axis=1, keepdims=True)
            )
            old = jnp.exp(old - highest)
            new = jnp.exp(new - highest)
            total = jnp.sum(old, axis=1, keepdims=True) + jnp.sum(new, axis=1, keepdims=True)
            inverse = 1.0 / total
            result = jnp.dot(
                (old * inverse).astype(jnp.bfloat16), values, preferred_element_type=jnp.float32
            )
            result = result + jnp.dot(
                (new * inverse).astype(jnp.bfloat16),
                kvbuf[0:NEW, HEAD_DIM : 2 * HEAD_DIM],
                preferred_element_type=jnp.float32,
            )
            decoded_ref[r] = result.astype(jnp.bfloat16)

    doc_row = jnp.broadcast_to(documents_ref[...], (TRAIN_DEV, TRAIN_DEV))
    row_id = lax.broadcasted_iota(jnp.int32, (TRAIN_DEV, TRAIN_DEV), 0)
    col_id = lax.broadcasted_iota(jnp.int32, (TRAIN_DEV, TRAIN_DEV), 1)
    doc_col = jnp.sum(jnp.where(row_id == col_id, doc_row, 0), axis=1, keepdims=True)
    train_mask = (col_id <= row_id) & (doc_row == doc_col)

    def train(heads):
        for g in heads:
            span = slice(g * HEAD_DIM, (g + 1) * HEAD_DIM)
            values = dot_nt(train_queries_ref[:, span], kvbuf[NEW:, 0:HEAD_DIM]) * SCALE
            values = jnp.where(train_mask, values, MASKED)
            expo = jnp.exp(values - jnp.max(values, axis=1, keepdims=True))
            inverse = 1.0 / jnp.sum(expo, axis=1, keepdims=True)
            result = jnp.dot(
                (expo * inverse).astype(jnp.bfloat16),
                kvbuf[NEW:, HEAD_DIM : 2 * HEAD_DIM],
                preferred_element_type=jnp.float32,
            )
            train_out_ref[:, span] = result.astype(jnp.bfloat16)

    rows_z.start()
    rows_z.spread(0)
    decode(range(0, 2))
    rows_z.step(0, 1)
    decode(range(2, 4))
    rows_z.step(0, 2)
    rows_z.chain(1)
    rows_z.spread(1)
    rows_z.step(0, 3)
    decode(range(4, 6))
    rows_z.step(1, 1)
    decode(range(6, 8))
    rows_z.step(1, 2)
    rows_z.chain(2)
    rows_z.spread(2)
    rows_z.step(1, 3)
    decode(range(8, 10))
    rows_z.step(2, 1)
    decode(range(10, 12))
    rows_z.step(2, 2)
    rows_z.chain(3)
    rows_z.spread(3)
    rows_z.step(2, 3)
    decode(range(12, 16))
    rows_z.step(3, 1)
    train(range(0, 4))
    rows_z.step(3, 2)
    train(range(4, 8))
    rows_z.step(3, 3)

    out_row = lax.broadcasted_iota(jnp.int32, (64, 128), 0)
    in_row = lax.broadcasted_iota(jnp.int32, (64, 128), 1)
    owner = (z * (YS * CORES) + out_row // 8 + 1).astype(jnp.float32)
    same = ((out_row // 2) % PLACES == in_row // NEW) & (out_row % 2 == in_row % 2)
    pieces = []
    for rr in range(RUNS):
        asked = mbuf[rr, 0] + mbuf[rr, 1] + mbuf[rr, 2] + mbuf[rr, 3]
        chosen = jnp.where(same & (asked == owner), 1.0, 0.0).astype(jnp.bfloat16)
        rows = fbuf[rr].reshape(PLACES * NEW, COLS)
        pieces.append(jnp.dot(chosen, rows, preferred_element_type=jnp.float32))
    for o in range(YS * CORES):
        rows = jnp.concatenate([piece[o * 8 : (o + 1) * 8] for piece in pieces], axis=0)
        hstage[o] = rows.astype(jnp.bfloat16)
    for step in range(1, YS * CORES):
        target = (octet + step) % (YS * CORES)
        send(
            True,
            lambda step=step, target=target: remote(
                hstage.at[target],
                hrecv.at[octet],
                h_send.at[step],
                h_recv.at[octet],
                z * (YS * CORES) + target,
            ),
        )
    hrecv[octet] = hstage[octet]
    settle()
    for step in range(1, YS * CORES):
        source = (octet + step) % (YS * CORES)
        remote(
            hstage.at[source],
            hrecv.at[source],
            h_send.at[step],
            h_recv.at[source],
            z * (YS * CORES) + source,
        ).wait_recv()
    handover_ref[...] = hrecv[...]


def local(
    new_hidden,
    new_queries,
    paged_cache,
    block_table,
    lengths,
    destination,
    train_hidden,
    train_queries,
    documents,
    project_weight,
    project_bias,
):
    vmem = pl.BlockSpec(memory_space=pltpu.VMEM)
    smem = pl.BlockSpec(memory_space=pltpu.SMEM)
    anywhere = pl.BlockSpec(memory_space=pl.ANY)
    dma = pltpu.SemaphoreType.DMA
    along = [dma((2, RUNS)), dma((RUNS,)), dma((2, RUNS, PLACES)), dma((RUNS, PLACES))]
    decoded, attended, handed = pl.pallas_call(
        kernel,
        out_shape=(
            jax.ShapeDtypeStruct((ROWS_DEV, CORES * GROUP, HEAD_DIM), jnp.bfloat16),
            jax.ShapeDtypeStruct((TRAIN_DEV, GROUP * HEAD_DIM), jnp.bfloat16),
            jax.ShapeDtypeStruct((YS * CORES, RUNS * PLACES * 2, COLS), jnp.bfloat16),
        ),
        in_specs=[smem, smem, smem, vmem, vmem, vmem, vmem] + [anywhere] * 4,
        out_specs=(vmem, vmem, vmem),
        scratch_shapes=[
            pltpu.VMEM((YS, RUNS, PLACES, CORES, BLOCK, COLS), jnp.bfloat16),
            pltpu.VMEM((NEW + TRAIN_DEV, WIDTH), jnp.bfloat16),
            pltpu.VMEM((paged_cache.shape[0], PAGE, COLS), jnp.bfloat16),
            pltpu.VMEM((RUNS, PLACES, 1, 128), jnp.float32),
            pltpu.VMEM((RUNS, PLACES, NEW, COLS), jnp.bfloat16),
            pltpu.VMEM((NEW + TRAIN_DEV, COLS), jnp.float32),
            pltpu.VMEM((NEW + TRAIN_DEV, COLS), jnp.bfloat16),
            pltpu.VMEM((ROWS_DEV, CORES * GROUP, CONTEXT), jnp.float32),
            pltpu.VMEM((YS * CORES, RUNS * PLACES * 2, COLS), jnp.bfloat16),
            pltpu.VMEM((YS * CORES, RUNS * PLACES * 2, COLS), jnp.bfloat16),
            dma((4,)),
            *along,
            *along,
            *along,
            dma((2, RUNS)),
            dma((RUNS,)),
            dma((YS, RUNS)),
            dma((YS, RUNS)),
            dma((YS, RUNS)),
            dma((YS * CORES,)),
            dma((YS * CORES,)),
        ],
        compiler_params=pltpu.CompilerParams(collective_id=0, has_side_effects=True),
    )(
        block_table,
        lengths,
        destination,
        documents,
        project_bias.reshape(1, COLS),
        new_queries.reshape(ROWS_DEV, 2 * GROUP, HEAD_DIM),
        train_queries,
        new_hidden.reshape(NEW, WIDTH),
        train_hidden,
        paged_cache,
        project_weight,
    )
    decoded = decoded.reshape(ROWS_DEV, 2, GROUP * HEAD_DIM)
    handed = handed.reshape(YS * CORES, RUNS * PLACES, 2, COLS).transpose(1, 0, 2, 3)
    return decoded, attended, handed.reshape(RUNS * PLACES * YS * CORES, 2, COLS)


def solution(mesh):
    return jax.shard_map(
        local,
        mesh=mesh,
        in_specs=(
            P("fsdp", None, None),
            P("fsdp", None, "tensor"),
            P("fsdp", None, "tensor"),
            P("fsdp", None),
            P("fsdp"),
            P("fsdp"),
            P("fsdp", None),
            P("fsdp", "tensor"),
            P("fsdp", None),
            P("fsdp", "tensor"),
            P("tensor"),
        ),
        out_specs=(P("fsdp", None, "tensor"), P("fsdp", "tensor"), P("fsdp", None, "tensor")),
        check_vma=False,
    )
```

```python
import jax
import jax.numpy as jnp
from jax import lax
from jax.experimental import pallas as pl
from jax.experimental.pallas import tpu as pltpu
from jax.sharding import PartitionSpec as P

HEADS = 64
KV_HEADS = 8
HEAD_DIM = 128
GROUP = HEADS // KV_HEADS
MESH = pl.DeviceIdType.MESH
SCALE = HEAD_DIM ** (-0.5)
MASKED = -1e30

RUNS = 4
PLACES = 4
YS = 4
CORES = 2
ROWS_DEV = 16
TRAIN_DEV = 64
BLOCK = 64
WIDTH = 8192
COLS = 256
PAGE = 64
MAX_PAGES = 8
CONTEXT = PAGE * MAX_PAGES
NEW = ROWS_DEV * 2
ALL_ROWS = NEW + TRAIN_DEV
LANES = CORES * BLOCK
RELAY_CHAIN = False
RELAY_GROUP = True


def dot_nt(a, b):
    return lax.dot_general(a, b, (((1,), (1,)), ((), ())), preferred_element_type=jnp.float32)


def kernel(
    table_ref,
    length_ref,
    destination_ref,
    documents_ref,
    bias_ref,
    queries_ref,
    train_queries_ref,
    new_hidden_hbm,
    train_hidden_hbm,
    cache_hbm,
    weight_hbm,
    decoded_ref,
    train_out_ref,
    handover_ref,
    wbuf,
    hbuf,
    raw,
    qbuf,
    pool,
    mbuf,
    fbuf,
    gbuf,
    acc,
    rbuf,
    kvbuf,
    scores,
    hstage,
    hrecv,
    local_sem,
    w_chain_send,
    w_chain_recv,
    w_group_send,
    w_group_recv,
    m_chain_send,
    m_chain_recv,
    m_group_send,
    m_group_recv,
    f_chain_send,
    f_chain_recv,
    f_group_send,
    f_group_recv,
    relay_send,
    own_sem,
    y_send,
    y_recv,
    r_send,
    r_recv,
    p_send,
    p_recv,
    h_send,
    h_recv,
):
    me = lax.axis_index("fsdp")
    core = me % CORES
    y = (me // CORES) % YS
    z = me // (CORES * YS)
    place = z % PLACES
    run = z // PLACES
    other = 1 - core
    octet = y * CORES + core

    def device(zz, yy, cc):
        return (zz * YS + yy) * CORES + cc

    def remote(src, dst, ssem, rsem, target):
        return pltpu.make_async_remote_copy(
            src_ref=src,
            dst_ref=dst,
            send_sem=ssem,
            recv_sem=rsem,
            device_id={"fsdp": target},
            device_id_type=MESH,
        )

    def when(cond, do):
        if cond is True:
            do()
        else:
            pl.when(cond)(do)

    def both(a, b):
        if a is True:
            return b
        if b is True:
            return a
        return jnp.logical_and(a, b)

    pending = []

    def send(cond, make):
        when(cond, lambda: make().start())
        pending.append((cond, make))

    def settle():
        for cond, make in pending:
            when(cond, lambda make=make: make().wait_send())
        pending.clear()

    own_w = wbuf.at[run, place, core]
    w_copy = pltpu.make_async_copy(weight_hbm, own_w, local_sem.at[0])
    pool_copy = pltpu.make_async_copy(cache_hbm, pool, local_sem.at[1])
    new_copy = pltpu.make_async_copy(new_hidden_hbm, raw, local_sem.at[2])
    train_copy = pltpu.make_async_copy(
        train_hidden_hbm, hbuf.at[pl.ds(NEW, TRAIN_DEV)], local_sem.at[3]
    )
    w_copy.start()
    pool_copy.start()
    new_copy.start()
    train_copy.start()

    lane = lax.broadcasted_iota(jnp.int32, (1, 128), 1)
    wanted = jnp.zeros((1, 128), jnp.float32)
    for r in range(ROWS_DEV):
        value = (destination_ref[r] + 1).astype(jnp.float32)
        hit = (lane // NEW == place) & ((lane % NEW) // 2 == r)
        wanted = jnp.where(hit, value, wanted)
    mbuf[run, place] = wanted

    barrier = pltpu.get_barrier_semaphore()
    for step in range(1, YS * CORES):
        pl.semaphore_signal(
            barrier,
            inc=1,
            device_id={"fsdp": z * (YS * CORES) + (octet + step) % (YS * CORES)},
            device_id_type=MESH,
        )
    expected = jnp.int32(YS * CORES - 1)
    near = [
        (jnp.logical_and(run + side * far >= 0, run + side * far < RUNS), z + side * far * PLACES)
        for far in (1, 2, 3)
        for side in (1, -1)
    ] + [
        (jnp.logical_and(place + side * far >= 0, place + side * far < PLACES), z + side * far)
        for far in (1, 2, 3)
        for side in (1, -1)
    ]
    for cond, zz in near:

        @pl.when(cond)
        def _(zz=zz):
            pl.semaphore_signal(
                barrier, inc=1, device_id={"fsdp": device(zz, y, core)}, device_id_type=MESH
            )

        expected = expected + cond.astype(jnp.int32)
    for r in range(ROWS_DEV):
        both_tokens = queries_ref[r]
        qbuf[r] = jnp.concatenate(
            [both_tokens[:, g * HEAD_DIM : (g + 1) * HEAD_DIM] for g in range(GROUP)], axis=0
        )
    new_copy.wait()
    hbuf[0:NEW] = raw[...].reshape(NEW, WIDTH)
    pl.semaphore_wait(barrier, expected)

    class Along:
        def __init__(self, parts, relay=None):
            self.parts = parts
            self.relay = relay

        def start(self):
            for far in (2, 1) if self.relay is not None and RELAY_CHAIN else (3, 2, 1):
                for side in (1, -1):
                    target = run + side * far
                    cond = jnp.logical_and(target >= 0, target < RUNS)
                    for block, source, cs, cr, _, _ in self.parts:
                        src = block(run, place) if source is None else source
                        send(
                            cond,
                            lambda src=src, block=block, cs=cs, cr=cr, target=target: remote(
                                src,
                                block(run, place),
                                cs.at[target],
                                cr.at[run],
                                device(target * PLACES + place, y, core),
                            ),
                        )

        def chain(self, d):
            for cond, rr in quads(d):

                def do(rr=rr):
                    for block, _, cs, cr, _, _ in self.parts:
                        remote(
                            block(rr, place),
                            block(rr, place),
                            cs.at[rr],
                            cr.at[rr],
                            device(z, y, other),
                        ).wait_recv()

                when(cond, do)
                if d == 2 and self.relay is not None and RELAY_CHAIN:
                    onward = run + jnp.where(rr < run, 1, -1)
                    ahead = both(cond, jnp.logical_and(onward >= 0, onward < RUNS))
                    for i, (block, _, cs, cr, _, _) in enumerate(self.parts):
                        send(
                            ahead,
                            lambda rr=rr, i=i, block=block, cr=cr, onward=onward: remote(
                                block(rr, place),
                                block(rr, place),
                                self.relay.at[i, RUNS],
                                cr.at[rr],
                                device(onward * PLACES + place, y, core),
                            ),
                        )

        def spread(self, d):
            for cond, rr in quads(d):
                for far in (2, 1) if self.relay is not None and RELAY_GROUP else (3, 2, 1):
                    for side in (1, -1):
                        target = place + side * far
                        inside = both(cond, jnp.logical_and(target >= 0, target < PLACES))
                        for block, source, _, _, gs, gr in self.parts:
                            src = source if (d == 0 and source is not None) else block(rr, place)
                            send(
                                inside,
                                lambda src=src, block=block, gs=gs, gr=gr, rr=rr, target=target: (
                                    remote(
                                        src,
                                        block(rr, place),
                                        gs.at[rr, target],
                                        gr.at[rr, place],
                                        device(run * PLACES + target, y, core),
                                    )
                                ),
                            )

        def gather(self, d):
            for far in (2, 1, 3):
                for side in (1, -1):
                    pp = place + side * far
                    for cond, rr in quads(d):
                        inside = both(cond, jnp.logical_and(pp >= 0, pp < PLACES))

                        def do(rr=rr, pp=pp):
                            for block, _, _, _, gs, gr in self.parts:
                                remote(
                                    block(rr, pp),
                                    block(rr, pp),
                                    gs.at[rr, pp],
                                    gr.at[rr, pp],
                                    device(z, y, other),
                                ).wait_recv()

                        when(inside, do)
                        if far == 2 and self.relay is not None and RELAY_GROUP:
                            onward = place - side
                            ahead = both(
                                inside, jnp.logical_and(onward >= 0, onward < PLACES)
                            )
                            for i, (block, _, _, _, _, gr) in enumerate(self.parts):
                                send(
                                    ahead,
                                    lambda rr=rr, pp=pp, i=i, block=block, gr=gr, onward=onward: (
                                        remote(
                                            block(rr, pp),
                                            block(rr, pp),
                                            self.relay.at[i, rr],
                                            gr.at[rr, pp],
                                            device(run * PLACES + onward, y, core),
                                        )
                                    ),
                                )

    def quads(d):
        if d == 0:
            return [(True, run)]
        return [(run - d >= 0, run - d), (run + d < RUNS, run + d)]

    weights = Along(
        [
            (
                lambda rr, pp: wbuf.at[rr, pp, core],
                weight_hbm,
                w_chain_send,
                w_chain_recv,
                w_group_send,
                w_group_recv,
            ),
            (
                lambda rr, pp: mbuf.at[rr, pp],
                None,
                m_chain_send,
                m_chain_recv,
                m_group_send,
                m_group_recv,
            ),
        ],
        relay_send,
    )

    def pass_over(cond, rr):
        send(
            cond,
            lambda: remote(
                wbuf.at[rr, :, core],
                wbuf.at[rr, :, core],
                p_send.at[rr],
                p_recv.at[rr],
                device(z, y, other),
            ),
        )

    def chained(d):
        weights.chain(d)
        weights.spread(d)

    def gathered(d):
        weights.gather(d)
        for cond, rr in quads(d):
            pass_over(cond, rr)

    def columns(rr, pp, yy):
        start = ((rr * PLACES + pp) * YS + yy) * LANES
        return hbuf.at[:, pl.ds(pl.multiple_of(start, LANES), LANES)]

    def hidden_slot(rr, pp, yy):
        return gbuf.at[rr, yy, :, pl.ds(pp * LANES, LANES)]

    def own_copy(rr, pp):
        return pltpu.make_async_copy(
            columns(rr, pp, y), hidden_slot(rr, pp, y), own_sem.at[rr, pp]
        )

    def hidden_out():
        for rr in range(RUNS):
            for turn in (2, 1, 3):
                yy = (y + turn) % YS
                for pp in range(PLACES):
                    send(
                        True,
                        lambda rr=rr, pp=pp, turn=turn, yy=yy: remote(
                            columns(rr, pp, yy),
                            hidden_slot(rr, pp, y),
                            y_send.at[turn, rr, pp],
                            y_recv.at[y, rr, pp],
                            device(z, yy, core),
                        ),
                    )
            for pp in range(PLACES):
                own_copy(rr, pp).start()

    def hidden_in():
        for rr in range(RUNS):
            for pp in range(PLACES):
                own_copy(rr, pp).wait()
                for turn in (1, 3, 2):
                    yy = (y + turn) % YS
                    landed = hidden_slot(rr, pp, yy)
                    remote(
                        landed,
                        landed,
                        y_send.at[turn, rr, pp],
                        y_recv.at[yy, rr, pp],
                        device(z, y, other),
                    ).wait_recv()

    def multiply(rr):
        landed = wbuf.at[rr, :, other]
        remote(landed, landed, p_send.at[rr], p_recv.at[rr], device(z, y, other)).wait_recv()
        left = gbuf[rr].reshape(YS * ALL_ROWS, PLACES * LANES)
        right = wbuf[rr].reshape(PLACES * LANES, COLS)
        product = jnp.dot(left, right, preferred_element_type=jnp.float32)
        acc[...] += product.reshape(YS, ALL_ROWS, COLS)

    def multiplied(d):
        for cond, rr in quads(d):
            when(cond, lambda rr=rr: multiply(rr))

    def share_rows(part):
        return pl.ds(0, NEW) if part == 0 else pl.ds(NEW, TRAIN_DEV)

    def shares_out(part):
        for turn in (2, 1, 3):
            yy = (y + turn) % YS
            send(
                True,
                lambda turn=turn, yy=yy: remote(
                    acc.at[yy, share_rows(part)],
                    rbuf.at[y, share_rows(part)],
                    r_send.at[part, turn],
                    r_recv.at[part, y],
                    device(z, yy, core),
                ),
            )

    def shares_in(part):
        total = acc[y, share_rows(part)] + bias_ref[...]
        for turn in (1, 3, 2):
            yy = (y + turn) % YS
            landed = rbuf.at[yy, share_rows(part)]
            remote(
                landed, landed, r_send.at[part, turn], r_recv.at[part, yy], device(z, y, other)
            ).wait_recv()
            total = total + rbuf[yy, share_rows(part)]
        return total.astype(jnp.bfloat16)

    position = lax.broadcasted_iota(jnp.int32, (1, CONTEXT), 1)

    def old_scores(rows):
        for r in rows:
            keys = jnp.concatenate(
                [pool[table_ref[p, r], :, 0:HEAD_DIM] for p in range(MAX_PAGES)], axis=0
            )
            values = dot_nt(qbuf[r], keys) * SCALE
            scores[r] = jnp.where(position < length_ref[r], values, MASKED)

    acc[...] = jnp.zeros_like(acc)
    weights.start()
    weights.spread(0)
    train_copy.wait()
    hidden_out()
    pool_copy.wait()
    old_scores(range(0, 16))
    w_copy.wait()
    chained(1)
    chained(2)
    gathered(0)
    chained(3)
    gathered(1)
    gathered(2)
    gathered(3)
    hidden_in()
    multiplied(0)
    multiplied(1)
    multiplied(2)
    multiplied(3)
    shares_out(0)
    fresh = shares_in(0)
    fbuf[run, place] = fresh
    kvbuf[0:NEW] = fresh

    rows_z = Along(
        [
            (
                lambda rr, pp: fbuf.at[rr, pp],
                None,
                f_chain_send,
                f_chain_recv,
                f_group_send,
                f_group_recv,
            )
        ]
    )

    new_column = lax.broadcasted_iota(jnp.int32, (CORES * GROUP, NEW), 1)
    new_token = lax.broadcasted_iota(jnp.int32, (CORES * GROUP, NEW), 0) % 2

    def decode(rows):
        for r in rows:
            values = jnp.concatenate(
                [pool[table_ref[p, r], :, HEAD_DIM : 2 * HEAD_DIM] for p in range(MAX_PAGES)],
                axis=0,
            )
            old = scores[r]
            new = dot_nt(qbuf[r], kvbuf[0:NEW, 0:HEAD_DIM]) * SCALE
            allowed = (new_column // 2 == r) & (new_column % 2 <= new_token)
            new = jnp.where(allowed, new, MASKED)
            highest = jnp.maximum(
                jnp.max(old, axis=1, keepdims=True), jnp.max(new, axis=1, keepdims=True)
            )
            old = jnp.exp(old - highest)
            new = jnp.exp(new - highest)
            total = jnp.sum(old, axis=1, keepdims=True) + jnp.sum(new, axis=1, keepdims=True)
            inverse = 1.0 / total
            result = jnp.dot(
                (old * inverse).astype(jnp.bfloat16), values, preferred_element_type=jnp.float32
            )
            result = result + jnp.dot(
                (new * inverse).astype(jnp.bfloat16),
                kvbuf[0:NEW, HEAD_DIM : 2 * HEAD_DIM],
                preferred_element_type=jnp.float32,
            )
            decoded_ref[r] = jnp.concatenate(
                [result[2 * g : 2 * g + 2] for g in range(GROUP)], axis=1
            ).astype(jnp.bfloat16)

    doc_row = jnp.broadcast_to(documents_ref[...], (TRAIN_DEV, TRAIN_DEV))
    row_id = lax.broadcasted_iota(jnp.int32, (TRAIN_DEV, TRAIN_DEV), 0)
    col_id = lax.broadcasted_iota(jnp.int32, (TRAIN_DEV, TRAIN_DEV), 1)
    doc_col = jnp.sum(jnp.where(row_id == col_id, doc_row, 0), axis=1, keepdims=True)
    train_mask = (col_id <= row_id) & (doc_row == doc_col)

    def train(heads):
        for g in heads:
            span = slice(g * HEAD_DIM, (g + 1) * HEAD_DIM)
            values = dot_nt(train_queries_ref[:, span], kvbuf[NEW:, 0:HEAD_DIM]) * SCALE
            values = jnp.where(train_mask, values, MASKED)
            expo = jnp.exp(values - jnp.max(values, axis=1, keepdims=True))
            inverse = 1.0 / jnp.sum(expo, axis=1, keepdims=True)
            result = jnp.dot(
                (expo * inverse).astype(jnp.bfloat16),
                kvbuf[NEW:, HEAD_DIM : 2 * HEAD_DIM],
                preferred_element_type=jnp.float32,
            )
            train_out_ref[:, span] = result.astype(jnp.bfloat16)

    rows_z.start()
    rows_z.spread(0)
    shares_out(1)
    decode(range(0, 8))
    rows_z.chain(1)
    rows_z.spread(1)
    decode(range(8, 14))
    rows_z.chain(2)
    rows_z.spread(2)
    decode(range(14, 16))
    kvbuf[NEW:] = shares_in(1)
    train(range(0, 4))
    rows_z.chain(3)
    rows_z.spread(3)
    train(range(4, 8))
    rows_z.gather(0)
    rows_z.gather(1)
    rows_z.gather(2)
    rows_z.gather(3)

    out_row = lax.broadcasted_iota(jnp.int32, (64, 128), 0)
    in_row = lax.broadcasted_iota(jnp.int32, (64, 128), 1)
    owner = (z * (YS * CORES) + out_row // 8 + 1).astype(jnp.float32)
    same = ((out_row // 2) % PLACES == in_row // NEW) & (out_row % 2 == in_row % 2)
    pieces = []
    for rr in range(RUNS):
        asked = mbuf[rr, 0] + mbuf[rr, 1] + mbuf[rr, 2] + mbuf[rr, 3]
        chosen = jnp.where(same & (asked == owner), 1.0, 0.0).astype(jnp.bfloat16)
        rows = fbuf[rr].reshape(PLACES * NEW, COLS)
        pieces.append(jnp.dot(chosen, rows, preferred_element_type=jnp.float32))
    for o in range(YS * CORES):
        rows = jnp.concatenate([piece[o * 8 : (o + 1) * 8] for piece in pieces], axis=0)
        hstage[o] = rows.astype(jnp.bfloat16)
    for step in range(1, YS * CORES):
        target = (octet + step) % (YS * CORES)
        send(
            True,
            lambda step=step, target=target: remote(
                hstage.at[target],
                hrecv.at[octet],
                h_send.at[step],
                h_recv.at[octet],
                z * (YS * CORES) + target,
            ),
        )
    hrecv[octet] = hstage[octet]
    settle()
    for step in range(1, YS * CORES):
        source = (octet + step) % (YS * CORES)
        remote(
            hstage.at[source],
            hrecv.at[source],
            h_send.at[step],
            h_recv.at[source],
            z * (YS * CORES) + source,
        ).wait_recv()
    handover_ref[...] = hrecv[...]


def local(
    new_hidden,
    new_queries,
    paged_cache,
    block_table,
    lengths,
    destination,
    train_hidden,
    train_queries,
    documents,
    project_weight,
    project_bias,
):
    vmem = pl.BlockSpec(memory_space=pltpu.VMEM)
    smem = pl.BlockSpec(memory_space=pltpu.SMEM)
    anywhere = pl.BlockSpec(memory_space=pl.ANY)
    dma = pltpu.SemaphoreType.DMA
    along = [dma((RUNS,)), dma((RUNS,)), dma((RUNS, PLACES)), dma((RUNS, PLACES))]
    decoded, attended, handed = pl.pallas_call(
        kernel,
        out_shape=(
            jax.ShapeDtypeStruct((ROWS_DEV, 2, GROUP * HEAD_DIM), jnp.bfloat16),
            jax.ShapeDtypeStruct((TRAIN_DEV, GROUP * HEAD_DIM), jnp.bfloat16),
            jax.ShapeDtypeStruct((YS * CORES, RUNS * PLACES * 2, COLS), jnp.bfloat16),
        ),
        in_specs=[smem, smem, smem, vmem, vmem, vmem, vmem] + [anywhere] * 4,
        out_specs=(vmem, vmem, vmem),
        scratch_shapes=[
            pltpu.VMEM((RUNS, PLACES, CORES, BLOCK, COLS), jnp.bfloat16),
            pltpu.VMEM((ALL_ROWS, WIDTH), jnp.bfloat16),
            pltpu.VMEM((ROWS_DEV, 2, WIDTH), jnp.bfloat16),
            pltpu.VMEM((ROWS_DEV, 2 * GROUP, HEAD_DIM), jnp.bfloat16),
            pltpu.VMEM((paged_cache.shape[0], PAGE, COLS), jnp.bfloat16),
            pltpu.VMEM((RUNS, PLACES, 1, 128), jnp.float32),
            pltpu.VMEM((RUNS, PLACES, NEW, COLS), jnp.bfloat16),
            pltpu.VMEM((RUNS, YS, ALL_ROWS, PLACES * LANES), jnp.bfloat16),
            pltpu.VMEM((YS, ALL_ROWS, COLS), jnp.float32),
            pltpu.VMEM((YS, ALL_ROWS, COLS), jnp.float32),
            pltpu.VMEM((ALL_ROWS, COLS), jnp.bfloat16),
            pltpu.VMEM((ROWS_DEV, CORES * GROUP, CONTEXT), jnp.float32),
            pltpu.VMEM((YS * CORES, RUNS * PLACES * 2, COLS), jnp.bfloat16),
            pltpu.VMEM((YS * CORES, RUNS * PLACES * 2, COLS), jnp.bfloat16),
            dma((4,)),
            *along,
            *along,
            *along,
            dma((2, RUNS + 1)),
            dma((RUNS, PLACES)),
            dma((YS, RUNS, PLACES)),
            dma((YS, RUNS, PLACES)),
            dma((2, YS)),
            dma((2, YS)),
            dma((RUNS,)),
            dma((RUNS,)),
            dma((YS * CORES,)),
            dma((YS * CORES,)),
        ],
        compiler_params=pltpu.CompilerParams(collective_id=0, has_side_effects=True),
    )(
        block_table.T,
        lengths,
        destination,
        documents,
        project_bias.reshape(1, COLS),
        new_queries,
        train_queries,
        new_hidden,
        train_hidden,
        paged_cache,
        project_weight,
    )
    handed = handed.reshape(YS * CORES, RUNS * PLACES, 2, COLS).transpose(1, 0, 2, 3)
    return decoded, attended, handed.reshape(RUNS * PLACES * YS * CORES, 2, COLS)


def solution(mesh):
    return jax.shard_map(
        local,
        mesh=mesh,
        in_specs=(
            P("fsdp", None, None),
            P("fsdp", None, "tensor"),
            P("fsdp", None, "tensor"),
            P("fsdp", None),
            P("fsdp"),
            P("fsdp"),
            P("fsdp", None),
            P("fsdp", "tensor"),
            P("fsdp", None),
            P("fsdp", "tensor"),
            P("tensor"),
        ),
        out_specs=(P("fsdp", None, "tensor"), P("fsdp", "tensor"), P("fsdp", None, "tensor")),
        check_vma=False,
    )
```

```python
import jax
import jax.numpy as jnp
from jax import lax
from jax.experimental import pallas as pl
from jax.experimental.pallas import tpu as pltpu
from jax.sharding import PartitionSpec as P

HEADS = 64
KV_HEADS = 8
HEAD_DIM = 128
GROUP = HEADS // KV_HEADS
MESH = pl.DeviceIdType.MESH
SCALE = HEAD_DIM ** (-0.5)
MASKED = -1e30

RUNS = 4
PLACES = 4
YS = 4
CORES = 2
ROWS_DEV = 16
TRAIN_DEV = 64
BLOCK = 64
WIDTH = 8192
COLS = 256
PAGE = 64
MAX_PAGES = 8
CONTEXT = PAGE * MAX_PAGES
NEW = ROWS_DEV * 2
ALL_ROWS = NEW + TRAIN_DEV
LANES = CORES * BLOCK
NEAR = PLACES * YS * CORES
RELAY_CHAIN = False
RELAY_GROUP = True


def dot_nt(a, b):
    return lax.dot_general(a, b, (((1,), (1,)), ((), ())), preferred_element_type=jnp.float32)


def kernel(
    table_hbm,
    length_hbm,
    destination_hbm,
    documents_hbm,
    bias_hbm,
    queries_hbm,
    train_queries_hbm,
    new_hidden_hbm,
    train_hidden_hbm,
    cache_hbm,
    weight_hbm,
    decoded_ref,
    train_out_ref,
    handover_ref,
    table_ref,
    length_ref,
    destination_ref,
    documents_ref,
    bias_ref,
    queries_ref,
    train_queries_ref,
    wbuf,
    hbuf,
    raw,
    qbuf,
    pool,
    mbuf,
    fbuf,
    gbuf,
    acc,
    rbuf,
    kvbuf,
    scores,
    hstage,
    hrecv,
    local_sem,
    w_chain_send,
    w_chain_recv,
    w_group_send,
    w_group_recv,
    m_chain_send,
    m_chain_recv,
    f_chain_send,
    f_chain_recv,
    relay_send,
    own_sem,
    y_send,
    y_recv,
    r_send,
    r_recv,
    p_send,
    p_recv,
    h_send,
    h_recv,
):
    me = lax.axis_index("fsdp")
    core = me % CORES
    y = (me // CORES) % YS
    z = me // (CORES * YS)
    place = z % PLACES
    run = z // PLACES
    other = 1 - core
    octet = y * CORES + core

    def device(zz, yy, cc):
        return (zz * YS + yy) * CORES + cc

    def remote(src, dst, ssem, rsem, target):
        return pltpu.make_async_remote_copy(
            src_ref=src,
            dst_ref=dst,
            send_sem=ssem,
            recv_sem=rsem,
            device_id={"fsdp": target},
            device_id_type=MESH,
        )

    def when(cond, do):
        if cond is True:
            do()
        else:
            pl.when(cond)(do)

    def both(a, b):
        if a is True:
            return b
        if b is True:
            return a
        return jnp.logical_and(a, b)

    pending = []

    def send(cond, make):
        when(cond, lambda: make().start())
        pending.append((cond, make))

    def settle():
        for cond, make in pending:
            when(cond, lambda make=make: make().wait_send())
        pending.clear()

    own_w = wbuf.at[run, place, core]
    w_copy = pltpu.make_async_copy(weight_hbm, own_w, local_sem.at[0])
    pool_copy = pltpu.make_async_copy(cache_hbm, pool, local_sem.at[1])
    new_copy = pltpu.make_async_copy(new_hidden_hbm, raw, local_sem.at[2])
    train_copy = pltpu.make_async_copy(
        train_hidden_hbm, hbuf.at[pl.ds(NEW, TRAIN_DEV)], local_sem.at[3]
    )
    small_copies = [
        pltpu.make_async_copy(src, dst, local_sem.at[4 + i])
        for i, (src, dst) in enumerate(
            (
                (destination_hbm, destination_ref),
                (queries_hbm, queries_ref),
                (table_hbm, table_ref),
                (length_hbm, length_ref),
                (documents_hbm, documents_ref),
                (bias_hbm, bias_ref),
                (train_queries_hbm, train_queries_ref),
            )
        )
    ]
    barrier = pltpu.get_barrier_semaphore()
    here = place * (YS * CORES) + octet
    for step in range(1, NEAR):
        pl.semaphore_signal(
            barrier,
            inc=1,
            device_id={"fsdp": run * NEAR + (here + step) % NEAR},
            device_id_type=MESH,
        )
    for step in range(1, RUNS):
        pl.semaphore_signal(
            barrier,
            inc=1,
            device_id={"fsdp": ((run + step) % RUNS) * NEAR + here},
            device_id_type=MESH,
        )
    expected = NEAR + RUNS - 2
    w_copy.start()
    new_copy.start()
    for copy in small_copies:
        copy.start()
    train_copy.start()
    pool_copy.start()
    small_copies[0].wait()
    lane = lax.broadcasted_iota(jnp.int32, (1, 128), 1)
    wanted = jnp.zeros((1, 128), jnp.float32)
    for r in range(ROWS_DEV):
        value = (destination_ref[r] + 1).astype(jnp.float32)
        hit = (lane // NEW == run) & ((lane % NEW) // 2 == r)
        wanted = jnp.where(hit, value, wanted)
    mbuf[run] = wanted

    small_copies[1].wait()
    for r in range(ROWS_DEV):
        both_tokens = queries_ref[r]
        qbuf[r] = jnp.concatenate(
            [both_tokens[:, g * HEAD_DIM : (g + 1) * HEAD_DIM] for g in range(GROUP)], axis=0
        )
    new_copy.wait()
    hbuf[0:NEW] = raw[...].reshape(NEW, WIDTH)
    pl.semaphore_wait(barrier, expected)

    class Along:
        def __init__(self, parts, relay=None):
            self.parts = parts
            self.relay = relay

        def start(self):
            for far in (2, 1) if self.relay is not None and RELAY_CHAIN else (3, 2, 1):
                for side in (1, -1):
                    target = run + side * far
                    cond = jnp.logical_and(target >= 0, target < RUNS)
                    for block, source, cs, cr, _, _ in self.parts:
                        src = block(run, place) if source is None else source
                        send(
                            cond,
                            lambda src=src, block=block, cs=cs, cr=cr, target=target: remote(
                                src,
                                block(run, place),
                                cs.at[target],
                                cr.at[run],
                                device(target * PLACES + place, y, core),
                            ),
                        )

        def chain(self, d):
            for cond, rr in quads(d):

                def do(rr=rr):
                    for block, _, cs, cr, _, _ in self.parts:
                        remote(
                            block(rr, place),
                            block(rr, place),
                            cs.at[rr],
                            cr.at[rr],
                            device(z, y, other),
                        ).wait_recv()

                when(cond, do)
                if d == 2 and self.relay is not None and RELAY_CHAIN:
                    onward = run + jnp.where(rr < run, 1, -1)
                    ahead = both(cond, jnp.logical_and(onward >= 0, onward < RUNS))
                    for i, (block, _, cs, cr, _, _) in enumerate(self.parts):
                        send(
                            ahead,
                            lambda rr=rr, i=i, block=block, cr=cr, onward=onward: remote(
                                block(rr, place),
                                block(rr, place),
                                self.relay.at[i, RUNS],
                                cr.at[rr],
                                device(onward * PLACES + place, y, core),
                            ),
                        )

        def spread(self, d):
            for cond, rr in quads(d):
                for far in (2, 1) if self.relay is not None and RELAY_GROUP else (3, 2, 1):
                    for side in (1, -1):
                        target = place + side * far
                        inside = both(cond, jnp.logical_and(target >= 0, target < PLACES))
                        for block, source, _, _, gs, gr in self.parts[:1]:
                            src = source if (d == 0 and source is not None) else block(rr, place)
                            send(
                                inside,
                                lambda src=src, block=block, gs=gs, gr=gr, rr=rr, target=target: (
                                    remote(
                                        src,
                                        block(rr, place),
                                        gs.at[rr, target],
                                        gr.at[rr, place],
                                        device(run * PLACES + target, y, core),
                                    )
                                ),
                            )

        def gather(self, d):
            for far in (2, 1, 3):
                for side in (1, -1):
                    pp = place + side * far
                    for cond, rr in quads(d):
                        inside = both(cond, jnp.logical_and(pp >= 0, pp < PLACES))

                        def do(rr=rr, pp=pp):
                            for block, _, _, _, gs, gr in self.parts[:1]:
                                remote(
                                    block(rr, pp),
                                    block(rr, pp),
                                    gs.at[rr, pp],
                                    gr.at[rr, pp],
                                    device(z, y, other),
                                ).wait_recv()

                        when(inside, do)
                        if far == 2 and self.relay is not None and RELAY_GROUP:
                            onward = place - side
                            ahead = both(
                                inside, jnp.logical_and(onward >= 0, onward < PLACES)
                            )
                            for i, (block, _, _, _, _, gr) in enumerate(self.parts[:1]):
                                send(
                                    ahead,
                                    lambda rr=rr, pp=pp, i=i, block=block, gr=gr, onward=onward: (
                                        remote(
                                            block(rr, pp),
                                            block(rr, pp),
                                            self.relay.at[i, rr],
                                            gr.at[rr, pp],
                                            device(run * PLACES + onward, y, core),
                                        )
                                    ),
                                )

    def quads(d):
        if d == 0:
            return [(True, run)]
        return [(run - d >= 0, run - d), (run + d < RUNS, run + d)]

    weights = Along(
        [
            (
                lambda rr, pp: wbuf.at[rr, pp, core],
                weight_hbm,
                w_chain_send,
                w_chain_recv,
                w_group_send,
                w_group_recv,
            ),
            (
                lambda rr, pp: mbuf.at[rr],
                None,
                m_chain_send,
                m_chain_recv,
                None,
                None,
            ),
        ],
        relay_send,
    )

    def pass_over(cond, rr):
        send(
            cond,
            lambda: remote(
                wbuf.at[rr, :, core],
                wbuf.at[rr, :, core],
                p_send.at[rr],
                p_recv.at[rr],
                device(z, y, other),
            ),
        )

    def chained(d):
        weights.chain(d)
        weights.spread(d)

    def gathered(d):
        weights.gather(d)
        for cond, rr in quads(d):
            pass_over(cond, rr)

    def columns(rr, pp, yy):
        start = ((rr * PLACES + pp) * YS + yy) * LANES
        return hbuf.at[:, pl.ds(pl.multiple_of(start, LANES), LANES)]

    def hidden_slot(rr, pp, yy):
        return gbuf.at[rr, yy, :, pl.ds(pp * LANES, LANES)]

    def own_copy(rr, pp):
        return pltpu.make_async_copy(
            columns(rr, pp, y), hidden_slot(rr, pp, y), own_sem.at[rr, pp]
        )

    def hidden_out():
        for rr in range(RUNS):
            for turn in (2, 1, 3):
                yy = (y + turn) % YS
                for pp in range(PLACES):
                    send(
                        True,
                        lambda rr=rr, pp=pp, turn=turn, yy=yy: remote(
                            columns(rr, pp, yy),
                            hidden_slot(rr, pp, y),
                            y_send.at[turn, rr, pp],
                            y_recv.at[y, rr, pp],
                            device(z, yy, core),
                        ),
                    )
            for pp in range(PLACES):
                own_copy(rr, pp).start()

    def hidden_in():
        for rr in range(RUNS):
            for pp in range(PLACES):
                own_copy(rr, pp).wait()
                for turn in (1, 3, 2):
                    yy = (y + turn) % YS
                    landed = hidden_slot(rr, pp, yy)
                    remote(
                        landed,
                        landed,
                        y_send.at[turn, rr, pp],
                        y_recv.at[yy, rr, pp],
                        device(z, y, other),
                    ).wait_recv()

    def multiply(rr):
        landed = wbuf.at[rr, :, other]
        remote(landed, landed, p_send.at[rr], p_recv.at[rr], device(z, y, other)).wait_recv()
        left = gbuf[rr].reshape(YS * ALL_ROWS, PLACES * LANES)
        right = wbuf[rr].reshape(PLACES * LANES, COLS)
        product = jnp.dot(left, right, preferred_element_type=jnp.float32)
        acc[...] += product.reshape(YS, ALL_ROWS, COLS)

    def multiplied(d):
        for cond, rr in quads(d):
            when(cond, lambda rr=rr: multiply(rr))

    def share_rows(part):
        return pl.ds(0, NEW) if part == 0 else pl.ds(NEW, TRAIN_DEV)

    def shares_out(part):
        for turn in (2, 1, 3):
            yy = (y + turn) % YS
            send(
                True,
                lambda turn=turn, yy=yy: remote(
                    acc.at[yy, share_rows(part)],
                    rbuf.at[y, share_rows(part)],
                    r_send.at[part, turn],
                    r_recv.at[part, y],
                    device(z, yy, core),
                ),
            )

    def shares_in(part):
        total = acc[y, share_rows(part)] + bias_ref[...]
        for turn in (1, 3, 2):
            yy = (y + turn) % YS
            landed = rbuf.at[yy, share_rows(part)]
            remote(
                landed, landed, r_send.at[part, turn], r_recv.at[part, yy], device(z, y, other)
            ).wait_recv()
            total = total + rbuf[yy, share_rows(part)]
        return total.astype(jnp.bfloat16)

    position = lax.broadcasted_iota(jnp.int32, (1, CONTEXT), 1)

    def old_scores(rows):
        for r in rows:
            keys = jnp.concatenate(
                [pool[table_ref[p, r], :, 0:HEAD_DIM] for p in range(MAX_PAGES)], axis=0
            )
            values = dot_nt(qbuf[r], keys) * SCALE
            scores[r] = jnp.where(position < length_ref[r], values, MASKED)

    acc[...] = jnp.zeros_like(acc)
    weights.start()
    weights.spread(0)
    train_copy.wait()
    hidden_out()
    pool_copy.wait()
    for copy in small_copies[2:]:
        copy.wait()
    old_scores(range(0, 16))
    w_copy.wait()
    chained(1)
    chained(2)
    gathered(0)
    chained(3)
    gathered(1)
    gathered(2)
    hidden_in()
    multiplied(0)
    multiplied(1)
    gathered(3)
    multiplied(2)
    multiplied(3)
    shares_out(0)
    fresh = shares_in(0)
    fbuf[run] = fresh
    kvbuf[0:NEW] = fresh

    rows_z = Along(
        [
            (
                lambda rr, pp: fbuf.at[rr],
                None,
                f_chain_send,
                f_chain_recv,
                None,
                None,
            )
        ]
    )

    new_column = lax.broadcasted_iota(jnp.int32, (CORES * GROUP, NEW), 1)
    new_token = lax.broadcasted_iota(jnp.int32, (CORES * GROUP, NEW), 0) % 2

    def decode(rows):
        for r in rows:
            values = jnp.concatenate(
                [pool[table_ref[p, r], :, HEAD_DIM : 2 * HEAD_DIM] for p in range(MAX_PAGES)],
                axis=0,
            )
            old = scores[r]
            new = dot_nt(qbuf[r], kvbuf[0:NEW, 0:HEAD_DIM]) * SCALE
            allowed = (new_column // 2 == r) & (new_column % 2 <= new_token)
            new = jnp.where(allowed, new, MASKED)
            highest = jnp.maximum(
                jnp.max(old, axis=1, keepdims=True), jnp.max(new, axis=1, keepdims=True)
            )
            old = jnp.exp(old - highest)
            new = jnp.exp(new - highest)
            total = jnp.sum(old, axis=1, keepdims=True) + jnp.sum(new, axis=1, keepdims=True)
            inverse = 1.0 / total
            result = jnp.dot(
                (old * inverse).astype(jnp.bfloat16), values, preferred_element_type=jnp.float32
            )
            result = result + jnp.dot(
                (new * inverse).astype(jnp.bfloat16),
                kvbuf[0:NEW, HEAD_DIM : 2 * HEAD_DIM],
                preferred_element_type=jnp.float32,
            )
            decoded_ref[r] = jnp.concatenate(
                [result[2 * g : 2 * g + 2] for g in range(GROUP)], axis=1
            ).astype(jnp.bfloat16)

    doc_row = jnp.broadcast_to(documents_ref[...], (TRAIN_DEV, TRAIN_DEV))
    row_id = lax.broadcasted_iota(jnp.int32, (TRAIN_DEV, TRAIN_DEV), 0)
    col_id = lax.broadcasted_iota(jnp.int32, (TRAIN_DEV, TRAIN_DEV), 1)
    doc_col = jnp.sum(jnp.where(row_id == col_id, doc_row, 0), axis=1, keepdims=True)
    train_mask = (col_id <= row_id) & (doc_row == doc_col)

    def train(heads):
        for g in heads:
            span = slice(g * HEAD_DIM, (g + 1) * HEAD_DIM)
            values = dot_nt(train_queries_ref[:, span], kvbuf[NEW:, 0:HEAD_DIM]) * SCALE
            values = jnp.where(train_mask, values, MASKED)
            expo = jnp.exp(values - jnp.max(values, axis=1, keepdims=True))
            inverse = 1.0 / jnp.sum(expo, axis=1, keepdims=True)
            result = jnp.dot(
                (expo * inverse).astype(jnp.bfloat16),
                kvbuf[NEW:, HEAD_DIM : 2 * HEAD_DIM],
                preferred_element_type=jnp.float32,
            )
            train_out_ref[:, span] = result.astype(jnp.bfloat16)

    rows_z.start()
    shares_out(1)
    decode(range(0, 16))
    kvbuf[NEW:] = shares_in(1)
    train(range(0, 8))
    rows_z.chain(1)
    rows_z.chain(2)
    rows_z.chain(3)

    out_row = lax.broadcasted_iota(jnp.int32, (NEAR * RUNS * 2, RUNS * NEW), 0)
    in_row = lax.broadcasted_iota(jnp.int32, (NEAR * RUNS * 2, RUNS * NEW), 1)
    owner = (run * NEAR + out_row // (RUNS * 2) + 1).astype(jnp.float32)
    same = ((out_row // 2) % RUNS == in_row // NEW) & (out_row % 2 == in_row % 2)
    asked = mbuf[0] + mbuf[1] + mbuf[2] + mbuf[3]
    chosen = jnp.where(same & (asked == owner), 1.0, 0.0).astype(jnp.bfloat16)
    rows = jnp.dot(
        chosen, fbuf[...].reshape(RUNS * NEW, COLS), preferred_element_type=jnp.float32
    )
    hstage[...] = rows.astype(jnp.bfloat16).reshape(NEAR, RUNS, 2, COLS)
    for step in range(NEAR - 1, 0, -1):
        target = (here + step) % NEAR
        send(
            True,
            lambda step=step, target=target: remote(
                hstage.at[target],
                hrecv.at[:, here],
                h_send.at[step],
                h_recv.at[here],
                run * NEAR + target,
            ),
        )
    hrecv[:, here] = hstage[here]
    settle()
    for step in range(1, NEAR):
        source = (here + step) % NEAR
        remote(
            hstage.at[source],
            hrecv.at[:, source],
            h_send.at[step],
            h_recv.at[source],
            run * NEAR + source,
        ).wait_recv()
    handover_ref[...] = hrecv[...]


def finish(decoded, attended, handed, decoded_out, attended_out, handed_out):
    decoded_out[...] = decoded[...]
    attended_out[...] = attended[...]
    handed_out[...] = handed[...]


def local(
    new_hidden,
    new_queries,
    paged_cache,
    block_table,
    lengths,
    destination,
    train_hidden,
    train_queries,
    documents,
    project_weight,
    project_bias,
):
    vmem = pl.BlockSpec(memory_space=pltpu.VMEM)
    anywhere = pl.BlockSpec(memory_space=pl.ANY)
    dma = pltpu.SemaphoreType.DMA
    along = [dma((RUNS,)), dma((RUNS,)), dma((RUNS, PLACES)), dma((RUNS, PLACES))]
    decoded, attended, handed = pl.pallas_call(
        kernel,
        out_shape=(
            jax.ShapeDtypeStruct((ROWS_DEV, 2, GROUP * HEAD_DIM), jnp.bfloat16),
            jax.ShapeDtypeStruct((TRAIN_DEV, GROUP * HEAD_DIM), jnp.bfloat16),
            jax.ShapeDtypeStruct((RUNS, NEAR, 2, COLS), jnp.bfloat16),
        ),
        in_specs=[anywhere] * 11,
        out_specs=(vmem, vmem, vmem),
        scratch_shapes=[
            pltpu.SMEM((MAX_PAGES, ROWS_DEV), jnp.int32),
            pltpu.SMEM((ROWS_DEV,), jnp.int32),
            pltpu.SMEM((ROWS_DEV,), jnp.int32),
            pltpu.VMEM((1, TRAIN_DEV), jnp.int32),
            pltpu.VMEM((1, COLS), jnp.float32),
            pltpu.VMEM((ROWS_DEV, 2, GROUP * HEAD_DIM), jnp.bfloat16),
            pltpu.VMEM((TRAIN_DEV, GROUP * HEAD_DIM), jnp.bfloat16),
            pltpu.VMEM((RUNS, PLACES, CORES, BLOCK, COLS), jnp.bfloat16),
            pltpu.VMEM((ALL_ROWS, WIDTH), jnp.bfloat16),
            pltpu.VMEM((ROWS_DEV, 2, WIDTH), jnp.bfloat16),
            pltpu.VMEM((ROWS_DEV, 2 * GROUP, HEAD_DIM), jnp.bfloat16),
            pltpu.VMEM((paged_cache.shape[0], PAGE, COLS), jnp.bfloat16),
            pltpu.VMEM((RUNS, 1, 128), jnp.float32),
            pltpu.VMEM((RUNS, NEW, COLS), jnp.bfloat16),
            pltpu.VMEM((RUNS, YS, ALL_ROWS, PLACES * LANES), jnp.bfloat16),
            pltpu.VMEM((YS, ALL_ROWS, COLS), jnp.float32),
            pltpu.VMEM((YS, ALL_ROWS, COLS), jnp.float32),
            pltpu.VMEM((ALL_ROWS, COLS), jnp.bfloat16),
            pltpu.VMEM((ROWS_DEV, CORES * GROUP, CONTEXT), jnp.float32),
            pltpu.VMEM((NEAR, RUNS, 2, COLS), jnp.bfloat16),
            pltpu.VMEM((RUNS, NEAR, 2, COLS), jnp.bfloat16),
            dma((11,)),
            *along,
            dma((RUNS,)),
            dma((RUNS,)),
            dma((RUNS,)),
            dma((RUNS,)),
            dma((2, RUNS + 1)),
            dma((RUNS, PLACES)),
            dma((YS, RUNS, PLACES)),
            dma((YS, RUNS, PLACES)),
            dma((2, YS)),
            dma((2, YS)),
            dma((RUNS,)),
            dma((RUNS,)),
            dma((NEAR,)),
            dma((NEAR,)),
        ],
        compiler_params=pltpu.CompilerParams(collective_id=0, has_side_effects=True),
    )(
        block_table.T,
        lengths,
        destination,
        documents,
        project_bias.reshape(1, COLS),
        new_queries,
        train_queries,
        new_hidden,
        train_hidden,
        paged_cache,
        project_weight,
    )
    handed = handed.reshape(RUNS * PLACES * YS * CORES, 2, COLS)
    return pl.pallas_call(
        finish,
        out_shape=tuple(
            jax.ShapeDtypeStruct(x.shape, x.dtype) for x in (decoded, attended, handed)
        ),
        in_specs=[vmem] * 3,
        out_specs=(vmem,) * 3,
    )(decoded, attended, handed)


def solution(mesh):
    return jax.shard_map(
        local,
        mesh=mesh,
        in_specs=(
            P("fsdp", None, None),
            P("fsdp", None, "tensor"),
            P("fsdp", None, "tensor"),
            P("fsdp", None),
            P("fsdp"),
            P("fsdp"),
            P("fsdp", None),
            P("fsdp", "tensor"),
            P("fsdp", None),
            P("fsdp", "tensor"),
            P("tensor"),
        ),
        out_specs=(P("fsdp", None, "tensor"), P("fsdp", "tensor"), P("fsdp", None, "tensor")),
        check_vma=False,
    )
```

```python
import jax
import jax.numpy as jnp
from jax import lax
from jax.experimental import pallas as pl
from jax.experimental.pallas import tpu as pltpu
from jax.sharding import PartitionSpec as P

HEADS = 64
KV_HEADS = 8
HEAD_DIM = 128
GROUP = HEADS // KV_HEADS
MESH = pl.DeviceIdType.MESH
SCALE = HEAD_DIM ** (-0.5)
MASKED = -1e30

RUNS = 4
PLACES = 4
YS = 4
CORES = 2
ROWS_DEV = 16
TRAIN_DEV = 64
BLOCK = 64
WIDTH = 8192
COLS = 256
PAGE = 64
MAX_PAGES = 8
CONTEXT = PAGE * MAX_PAGES
NEW = ROWS_DEV * 2
ALL_ROWS = NEW + TRAIN_DEV
LANES = CORES * BLOCK
NEAR = PLACES * YS * CORES
RELAY_CHAIN = False
RELAY_GROUP = True


def dot_nt(a, b):
    return lax.dot_general(a, b, (((1,), (1,)), ((), ())), preferred_element_type=jnp.float32)


def kernel(
    table_hbm,
    length_hbm,
    destination_hbm,
    documents_hbm,
    bias_hbm,
    queries_hbm,
    train_queries_hbm,
    new_hidden_hbm,
    train_hidden_hbm,
    cache_hbm,
    weight_hbm,
    decoded_ref,
    train_out_ref,
    handover_ref,
    table_ref,
    length_ref,
    destination_ref,
    documents_ref,
    bias_ref,
    queries_ref,
    train_queries_ref,
    wbuf,
    hbuf,
    raw,
    qbuf,
    pool,
    mbuf,
    fbuf,
    gbuf,
    acc,
    rbuf,
    kvbuf,
    scores,
    hstage,
    hrecv,
    local_sem,
    w_chain_send,
    w_chain_recv,
    w_group_send,
    w_group_recv,
    m_chain_send,
    m_chain_recv,
    f_chain_send,
    f_chain_recv,
    relay_send,
    own_sem,
    y_send,
    y_recv,
    r_send,
    r_recv,
    p_send,
    p_recv,
    h_send,
    h_recv,
):
    me = lax.axis_index("fsdp")
    core = me % CORES
    y = (me // CORES) % YS
    z = me // (CORES * YS)
    place = z % PLACES
    run = z // PLACES
    other = 1 - core
    octet = y * CORES + core

    def device(zz, yy, cc):
        return (zz * YS + yy) * CORES + cc

    def remote(src, dst, ssem, rsem, target):
        return pltpu.make_async_remote_copy(
            src_ref=src,
            dst_ref=dst,
            send_sem=ssem,
            recv_sem=rsem,
            device_id={"fsdp": target},
            device_id_type=MESH,
        )

    def when(cond, do):
        if cond is True:
            do()
        else:
            pl.when(cond)(do)

    def both(a, b):
        if a is True:
            return b
        if b is True:
            return a
        return jnp.logical_and(a, b)

    pending = []

    def send(cond, make):
        when(cond, lambda: make().start())
        pending.append((cond, make))

    def settle(batch):
        for cond, make in batch:
            when(cond, lambda make=make: make().wait_send())

    own_w = wbuf.at[run, place, core]
    w_copy = pltpu.make_async_copy(weight_hbm, own_w, local_sem.at[0])
    pool_copy = pltpu.make_async_copy(cache_hbm, pool, local_sem.at[1])
    new_copy = pltpu.make_async_copy(new_hidden_hbm, raw, local_sem.at[2])
    train_copy = pltpu.make_async_copy(
        train_hidden_hbm, hbuf.at[pl.ds(NEW, TRAIN_DEV)], local_sem.at[3]
    )
    small_copies = [
        pltpu.make_async_copy(src, dst, local_sem.at[4 + i])
        for i, (src, dst) in enumerate(
            (
                (destination_hbm, destination_ref),
                (queries_hbm, queries_ref),
                (table_hbm, table_ref),
                (length_hbm, length_ref),
                (documents_hbm, documents_ref),
                (bias_hbm, bias_ref),
                (train_queries_hbm, train_queries_ref),
            )
        )
    ]
    barrier = pltpu.get_barrier_semaphore()
    here = place * (YS * CORES) + octet
    for step in range(1, NEAR):
        pl.semaphore_signal(
            barrier,
            inc=1,
            device_id={"fsdp": run * NEAR + (here + step) % NEAR},
            device_id_type=MESH,
        )
    for step in range(1, RUNS):
        pl.semaphore_signal(
            barrier,
            inc=1,
            device_id={"fsdp": ((run + step) % RUNS) * NEAR + here},
            device_id_type=MESH,
        )
    expected = NEAR + RUNS - 2
    w_copy.start()
    new_copy.start()
    for copy in small_copies:
        copy.start()
    train_copy.start()
    pool_copy.start()
    small_copies[0].wait()
    lane = lax.broadcasted_iota(jnp.int32, (1, 128), 1)
    wanted = jnp.zeros((1, 128), jnp.float32)
    for r in range(ROWS_DEV):
        value = (destination_ref[r] + 1).astype(jnp.float32)
        hit = (lane // NEW == run) & ((lane % NEW) // 2 == r)
        wanted = jnp.where(hit, value, wanted)
    mbuf[run] = wanted

    small_copies[1].wait()
    for r in range(ROWS_DEV):
        both_tokens = queries_ref[r]
        qbuf[r] = jnp.concatenate(
            [both_tokens[:, g * HEAD_DIM : (g + 1) * HEAD_DIM] for g in range(GROUP)], axis=0
        )
    new_copy.wait()
    hbuf[0:NEW] = raw[...].reshape(NEW, WIDTH)
    pl.semaphore_wait(barrier, expected)

    class Along:
        def __init__(self, parts, relay=None):
            self.parts = parts
            self.relay = relay

        def start(self):
            for far in (1, 2, 3) if self.relay is not None else (3, 2, 1):
                for side in (1, -1):
                    target = run + side * far
                    cond = jnp.logical_and(target >= 0, target < RUNS)
                    for block, source, cs, cr, _, _ in self.parts:
                        src = block(run, place) if source is None else source
                        send(
                            cond,
                            lambda src=src, block=block, cs=cs, cr=cr, target=target: remote(
                                src,
                                block(run, place),
                                cs.at[target],
                                cr.at[run],
                                device(target * PLACES + place, y, core),
                            ),
                        )

        def chain(self, d):
            for cond, rr in quads(d):

                def do(rr=rr):
                    for block, _, cs, cr, _, _ in self.parts:
                        remote(
                            block(rr, place),
                            block(rr, place),
                            cs.at[rr],
                            cr.at[rr],
                            device(z, y, other),
                        ).wait_recv()

                when(cond, do)
                if d == 2 and self.relay is not None and RELAY_CHAIN:
                    onward = run + jnp.where(rr < run, 1, -1)
                    ahead = both(cond, jnp.logical_and(onward >= 0, onward < RUNS))
                    for i, (block, _, cs, cr, _, _) in enumerate(self.parts):
                        send(
                            ahead,
                            lambda rr=rr, i=i, block=block, cr=cr, onward=onward: remote(
                                block(rr, place),
                                block(rr, place),
                                self.relay.at[i, RUNS],
                                cr.at[rr],
                                device(onward * PLACES + place, y, core),
                            ),
                        )

        def spread(self, d):
            for cond, rr in quads(d):
                for far in (2, 1) if self.relay is not None and RELAY_GROUP else (3, 2, 1):
                    for side in (1, -1):
                        target = place + side * far
                        inside = both(cond, jnp.logical_and(target >= 0, target < PLACES))
                        for block, source, _, _, gs, gr in self.parts[:1]:
                            src = source if (d == 0 and source is not None) else block(rr, place)
                            send(
                                inside,
                                lambda src=src, block=block, gs=gs, gr=gr, rr=rr, target=target: (
                                    remote(
                                        src,
                                        block(rr, place),
                                        gs.at[rr, target],
                                        gr.at[rr, place],
                                        device(run * PLACES + target, y, core),
                                    )
                                ),
                            )

        def gather(self, d):
            for far in (2, 1, 3):
                for side in (1, -1):
                    pp = place + side * far
                    for cond, rr in quads(d):
                        inside = both(cond, jnp.logical_and(pp >= 0, pp < PLACES))

                        def do(rr=rr, pp=pp):
                            for block, _, _, _, gs, gr in self.parts[:1]:
                                remote(
                                    block(rr, pp),
                                    block(rr, pp),
                                    gs.at[rr, pp],
                                    gr.at[rr, pp],
                                    device(z, y, other),
                                ).wait_recv()

                        when(inside, do)
                        if far == 2 and self.relay is not None and RELAY_GROUP:
                            onward = place - side
                            ahead = both(
                                inside, jnp.logical_and(onward >= 0, onward < PLACES)
                            )
                            for i, (block, _, _, _, _, gr) in enumerate(self.parts[:1]):
                                send(
                                    ahead,
                                    lambda rr=rr, pp=pp, i=i, block=block, gr=gr, onward=onward: (
                                        remote(
                                            block(rr, pp),
                                            block(rr, pp),
                                            self.relay.at[i, rr],
                                            gr.at[rr, pp],
                                            device(run * PLACES + onward, y, core),
                                        )
                                    ),
                                )

    def quads(d):
        if d == 0:
            return [(True, run)]
        return [(run - d >= 0, run - d), (run + d < RUNS, run + d)]

    weights = Along(
        [
            (
                lambda rr, pp: wbuf.at[rr, pp, core],
                weight_hbm,
                w_chain_send,
                w_chain_recv,
                w_group_send,
                w_group_recv,
            ),
            (
                lambda rr, pp: mbuf.at[rr],
                None,
                m_chain_send,
                m_chain_recv,
                None,
                None,
            ),
        ],
        relay_send,
    )

    def pass_over(cond, rr):
        send(
            cond,
            lambda: remote(
                wbuf.at[rr, :, core],
                wbuf.at[rr, :, core],
                p_send.at[rr],
                p_recv.at[rr],
                device(z, y, other),
            ),
        )

    def chained(d):
        weights.chain(d)
        weights.spread(d)

    def gathered(d):
        weights.gather(d)
        for cond, rr in quads(d):
            pass_over(cond, rr)

    def columns(rr, pp, yy):
        start = ((rr * PLACES + pp) * YS + yy) * LANES
        return hbuf.at[:, pl.ds(pl.multiple_of(start, LANES), LANES)]

    def hidden_slot(rr, pp, yy):
        return gbuf.at[rr, yy, :, pl.ds(pp * LANES, LANES)]

    def own_copy(rr, pp):
        return pltpu.make_async_copy(
            columns(rr, pp, y), hidden_slot(rr, pp, y), own_sem.at[rr, pp]
        )

    def hidden_out():
        for rr in range(RUNS):
            for turn in (2, 1, 3):
                yy = (y + turn) % YS
                for pp in range(PLACES):
                    send(
                        True,
                        lambda rr=rr, pp=pp, turn=turn, yy=yy: remote(
                            columns(rr, pp, yy),
                            hidden_slot(rr, pp, y),
                            y_send.at[turn, rr, pp],
                            y_recv.at[y, rr, pp],
                            device(z, yy, core),
                        ),
                    )
            for pp in range(PLACES):
                own_copy(rr, pp).start()

    def hidden_in():
        for rr in range(RUNS):
            for pp in range(PLACES):
                own_copy(rr, pp).wait()
                for turn in (1, 3, 2):
                    yy = (y + turn) % YS
                    landed = hidden_slot(rr, pp, yy)
                    remote(
                        landed,
                        landed,
                        y_send.at[turn, rr, pp],
                        y_recv.at[yy, rr, pp],
                        device(z, y, other),
                    ).wait_recv()

    def multiply(rr):
        landed = wbuf.at[rr, :, other]
        remote(landed, landed, p_send.at[rr], p_recv.at[rr], device(z, y, other)).wait_recv()
        left = gbuf[rr].reshape(YS * ALL_ROWS, PLACES * LANES)
        right = wbuf[rr].reshape(PLACES * LANES, COLS)
        product = jnp.dot(left, right, preferred_element_type=jnp.float32)
        acc[...] += product.reshape(YS, ALL_ROWS, COLS)

    def multiplied(d):
        for cond, rr in quads(d):
            when(cond, lambda rr=rr: multiply(rr))

    def share_rows(part):
        return pl.ds(0, NEW) if part == 0 else pl.ds(NEW, TRAIN_DEV)

    def shares_out(part):
        for turn in (2, 1, 3):
            yy = (y + turn) % YS
            send(
                True,
                lambda turn=turn, yy=yy: remote(
                    acc.at[yy, share_rows(part)],
                    rbuf.at[y, share_rows(part)],
                    r_send.at[part, turn],
                    r_recv.at[part, y],
                    device(z, yy, core),
                ),
            )

    def shares_in(part):
        total = acc[y, share_rows(part)] + bias_ref[...]
        for turn in (1, 3, 2):
            yy = (y + turn) % YS
            landed = rbuf.at[yy, share_rows(part)]
            remote(
                landed, landed, r_send.at[part, turn], r_recv.at[part, yy], device(z, y, other)
            ).wait_recv()
            total = total + rbuf[yy, share_rows(part)]
        return total.astype(jnp.bfloat16)

    position = lax.broadcasted_iota(jnp.int32, (1, CONTEXT), 1)

    def old_scores(rows):
        for r in rows:
            keys = jnp.concatenate(
                [pool[table_ref[p, r], :, 0:HEAD_DIM] for p in range(MAX_PAGES)], axis=0
            )
            values = dot_nt(qbuf[r], keys) * SCALE
            scores[r] = jnp.where(position < length_ref[r], values, MASKED)

    acc[...] = jnp.zeros_like(acc)
    weights.start()
    weights.spread(0)
    train_copy.wait()
    hidden_out()
    pool_copy.wait()
    for copy in small_copies[2:]:
        copy.wait()
    old_scores(range(0, 16))
    w_copy.wait()
    chained(1)
    chained(2)
    gathered(0)
    chained(3)
    gathered(1)
    gathered(2)
    hidden_in()
    multiplied(0)
    multiplied(1)
    gathered(3)
    multiplied(2)
    multiplied(3)
    shares_out(0)
    fresh = shares_in(0)
    fbuf[run] = fresh
    kvbuf[0:NEW] = fresh

    rows_z = Along(
        [
            (
                lambda rr, pp: fbuf.at[rr],
                None,
                f_chain_send,
                f_chain_recv,
                None,
                None,
            )
        ]
    )

    new_column = lax.broadcasted_iota(jnp.int32, (CORES * GROUP, NEW), 1)
    new_token = lax.broadcasted_iota(jnp.int32, (CORES * GROUP, NEW), 0) % 2

    def decode(rows):
        for r in rows:
            values = jnp.concatenate(
                [pool[table_ref[p, r], :, HEAD_DIM : 2 * HEAD_DIM] for p in range(MAX_PAGES)],
                axis=0,
            )
            old = scores[r]
            new = dot_nt(qbuf[r], kvbuf[0:NEW, 0:HEAD_DIM]) * SCALE
            allowed = (new_column // 2 == r) & (new_column % 2 <= new_token)
            new = jnp.where(allowed, new, MASKED)
            highest = jnp.maximum(
                jnp.max(old, axis=1, keepdims=True), jnp.max(new, axis=1, keepdims=True)
            )
            old = jnp.exp(old - highest)
            new = jnp.exp(new - highest)
            total = jnp.sum(old, axis=1, keepdims=True) + jnp.sum(new, axis=1, keepdims=True)
            inverse = 1.0 / total
            result = jnp.dot(
                (old * inverse).astype(jnp.bfloat16), values, preferred_element_type=jnp.float32
            )
            result = result + jnp.dot(
                (new * inverse).astype(jnp.bfloat16),
                kvbuf[0:NEW, HEAD_DIM : 2 * HEAD_DIM],
                preferred_element_type=jnp.float32,
            )
            decoded_ref[r] = jnp.concatenate(
                [result[2 * g : 2 * g + 2] for g in range(GROUP)], axis=1
            ).astype(jnp.bfloat16)

    doc_row = jnp.broadcast_to(documents_ref[...], (TRAIN_DEV, TRAIN_DEV))
    row_id = lax.broadcasted_iota(jnp.int32, (TRAIN_DEV, TRAIN_DEV), 0)
    col_id = lax.broadcasted_iota(jnp.int32, (TRAIN_DEV, TRAIN_DEV), 1)
    doc_col = jnp.sum(jnp.where(row_id == col_id, doc_row, 0), axis=1, keepdims=True)
    train_mask = (col_id <= row_id) & (doc_row == doc_col)

    def train(heads):
        for g in heads:
            span = slice(g * HEAD_DIM, (g + 1) * HEAD_DIM)
            values = dot_nt(train_queries_ref[:, span], kvbuf[NEW:, 0:HEAD_DIM]) * SCALE
            values = jnp.where(train_mask, values, MASKED)
            expo = jnp.exp(values - jnp.max(values, axis=1, keepdims=True))
            inverse = 1.0 / jnp.sum(expo, axis=1, keepdims=True)
            result = jnp.dot(
                (expo * inverse).astype(jnp.bfloat16),
                kvbuf[NEW:, HEAD_DIM : 2 * HEAD_DIM],
                preferred_element_type=jnp.float32,
            )
            train_out_ref[:, span] = result.astype(jnp.bfloat16)

    weight_sends = list(pending)
    pending.clear()
    rows_z.start()
    shares_out(1)
    decode(range(0, 16))
    kvbuf[NEW:] = shares_in(1)
    train(range(0, 8))
    settle(weight_sends)
    rows_z.chain(1)
    rows_z.chain(2)
    rows_z.chain(3)

    out_row = lax.broadcasted_iota(jnp.int32, (NEAR * RUNS * 2, RUNS * NEW), 0)
    in_row = lax.broadcasted_iota(jnp.int32, (NEAR * RUNS * 2, RUNS * NEW), 1)
    owner = (run * NEAR + out_row // (RUNS * 2) + 1).astype(jnp.float32)
    same = ((out_row // 2) % RUNS == in_row // NEW) & (out_row % 2 == in_row % 2)
    asked = mbuf[0] + mbuf[1] + mbuf[2] + mbuf[3]
    chosen = jnp.where(same & (asked == owner), 1.0, 0.0).astype(jnp.bfloat16)
    rows = jnp.dot(
        chosen, fbuf[...].reshape(RUNS * NEW, COLS), preferred_element_type=jnp.float32
    )
    hstage[...] = rows.astype(jnp.bfloat16).reshape(NEAR, RUNS, 2, COLS)
    for step in range(NEAR - 1, 0, -1):
        target = (here + step) % NEAR
        send(
            True,
            lambda step=step, target=target: remote(
                hstage.at[target],
                hrecv.at[:, here],
                h_send.at[step],
                h_recv.at[here],
                run * NEAR + target,
            ),
        )
    hrecv[:, here] = hstage[here]
    for step in range(1, NEAR):
        source = (here + step) % NEAR
        remote(
            hstage.at[source],
            hrecv.at[:, source],
            h_send.at[step],
            h_recv.at[source],
            run * NEAR + source,
        ).wait_recv()
    handover_ref[...] = hrecv[...]
    settle(pending)


def finish(decoded, attended, handed, decoded_out, attended_out, handed_out):
    decoded_out[...] = decoded[...]
    attended_out[...] = attended[...]
    handed_out[...] = handed[...]


def local(
    new_hidden,
    new_queries,
    paged_cache,
    block_table,
    lengths,
    destination,
    train_hidden,
    train_queries,
    documents,
    project_weight,
    project_bias,
):
    vmem = pl.BlockSpec(memory_space=pltpu.VMEM)
    hbm = pl.BlockSpec(memory_space=pltpu.HBM)
    dma = pltpu.SemaphoreType.DMA
    along = [dma((RUNS,)), dma((RUNS,)), dma((RUNS, PLACES)), dma((RUNS, PLACES))]
    decoded, attended, handed = pl.pallas_call(
        kernel,
        out_shape=(
            jax.ShapeDtypeStruct((ROWS_DEV, 2, GROUP * HEAD_DIM), jnp.bfloat16),
            jax.ShapeDtypeStruct((TRAIN_DEV, GROUP * HEAD_DIM), jnp.bfloat16),
            jax.ShapeDtypeStruct((RUNS, NEAR, 2, COLS), jnp.bfloat16),
        ),
        in_specs=[hbm] * 11,
        out_specs=(vmem, vmem, vmem),
        scratch_shapes=[
            pltpu.SMEM((MAX_PAGES, ROWS_DEV), jnp.int32),
            pltpu.SMEM((ROWS_DEV,), jnp.int32),
            pltpu.SMEM((ROWS_DEV,), jnp.int32),
            pltpu.VMEM((1, TRAIN_DEV), jnp.int32),
            pltpu.VMEM((1, COLS), jnp.float32),
            pltpu.VMEM((ROWS_DEV, 2, GROUP * HEAD_DIM), jnp.bfloat16),
            pltpu.VMEM((TRAIN_DEV, GROUP * HEAD_DIM), jnp.bfloat16),
            pltpu.VMEM((RUNS, PLACES, CORES, BLOCK, COLS), jnp.bfloat16),
            pltpu.VMEM((ALL_ROWS, WIDTH), jnp.bfloat16),
            pltpu.VMEM((ROWS_DEV, 2, WIDTH), jnp.bfloat16),
            pltpu.VMEM((ROWS_DEV, 2 * GROUP, HEAD_DIM), jnp.bfloat16),
            pltpu.VMEM((paged_cache.shape[0], PAGE, COLS), jnp.bfloat16),
            pltpu.VMEM((RUNS, 1, 128), jnp.float32),
            pltpu.VMEM((RUNS, NEW, COLS), jnp.bfloat16),
            pltpu.VMEM((RUNS, YS, ALL_ROWS, PLACES * LANES), jnp.bfloat16),
            pltpu.VMEM((YS, ALL_ROWS, COLS), jnp.float32),
            pltpu.VMEM((YS, ALL_ROWS, COLS), jnp.float32),
            pltpu.VMEM((ALL_ROWS, COLS), jnp.bfloat16),
            pltpu.VMEM((ROWS_DEV, CORES * GROUP, CONTEXT), jnp.float32),
            pltpu.VMEM((NEAR, RUNS, 2, COLS), jnp.bfloat16),
            pltpu.VMEM((RUNS, NEAR, 2, COLS), jnp.bfloat16),
            dma((11,)),
            *along,
            dma((RUNS,)),
            dma((RUNS,)),
            dma((RUNS,)),
            dma((RUNS,)),
            dma((2, RUNS + 1)),
            dma((RUNS, PLACES)),
            dma((YS, RUNS, PLACES)),
            dma((YS, RUNS, PLACES)),
            dma((2, YS)),
            dma((2, YS)),
            dma((RUNS,)),
            dma((RUNS,)),
            dma((NEAR,)),
            dma((NEAR,)),
        ],
        compiler_params=pltpu.CompilerParams(
            collective_id=0, has_side_effects=True, vmem_limit_bytes=24 * 1024 * 1024
        ),
    )(
        *(
            pltpu.with_memory_space_constraint(x, pltpu.HBM)
            for x in (
                block_table.T,
                lengths,
                destination,
                documents,
                project_bias.reshape(1, COLS),
                new_queries,
                train_queries,
                new_hidden,
                train_hidden,
                paged_cache,
                project_weight,
            )
        )
    )
    handed = handed.reshape(RUNS * PLACES * YS * CORES, 2, COLS)
    return pl.pallas_call(
        finish,
        out_shape=tuple(
            jax.ShapeDtypeStruct(x.shape, x.dtype) for x in (decoded, attended, handed)
        ),
        in_specs=[vmem] * 3,
        out_specs=(vmem,) * 3,
        compiler_params=pltpu.CompilerParams(vmem_limit_bytes=4 * 1024 * 1024),
    )(decoded, attended, handed)


def solution(mesh):
    return jax.shard_map(
        local,
        mesh=mesh,
        in_specs=(
            P("fsdp", None, None),
            P("fsdp", None, "tensor"),
            P("fsdp", None, "tensor"),
            P("fsdp", None),
            P("fsdp"),
            P("fsdp"),
            P("fsdp", None),
            P("fsdp", "tensor"),
            P("fsdp", None),
            P("fsdp", "tensor"),
            P("tensor"),
        ),
        out_specs=(P("fsdp", None, "tensor"), P("fsdp", "tensor"), P("fsdp", None, "tensor")),
        check_vma=False,
    )
```

```python
import jax
import jax.numpy as jnp
from jax import lax
from jax.experimental import pallas as pl
from jax.experimental.pallas import tpu as pltpu
from jax.sharding import PartitionSpec as P

HEADS = 64
KV_HEADS = 8
HEAD_DIM = 128
GROUP = HEADS // KV_HEADS
MESH = pl.DeviceIdType.MESH
SCALE = HEAD_DIM ** (-0.5)
MASKED = -1e30

RUNS = 4
PLACES = 4
YS = 4
CORES = 2
ROWS_DEV = 16
TRAIN_DEV = 64
BLOCK = 64
WIDTH = 8192
COLS = 256
PAGE = 64
MAX_PAGES = 8
CONTEXT = PAGE * MAX_PAGES
NEW = ROWS_DEV * 2
ALL_ROWS = NEW + TRAIN_DEV
LANES = CORES * BLOCK
NEAR = PLACES * YS * CORES
RELAY_CHAIN = False
RELAY_GROUP = True


def dot_nt(a, b):
    return lax.dot_general(a, b, (((1,), (1,)), ((), ())), preferred_element_type=jnp.float32)


def kernel(
    table_hbm,
    length_hbm,
    destination_hbm,
    documents_hbm,
    bias_hbm,
    queries_hbm,
    train_queries_hbm,
    new_hidden_hbm,
    train_hidden_hbm,
    cache_hbm,
    weight_hbm,
    decoded_ref,
    train_out_ref,
    handover_ref,
    table_ref,
    length_ref,
    destination_ref,
    documents_ref,
    bias_ref,
    queries_ref,
    train_queries_ref,
    wbuf,
    hbuf,
    raw,
    qbuf,
    pool,
    mbuf,
    fbuf,
    gbuf,
    acc,
    rbuf,
    kvbuf,
    scores,
    hstage,
    hrecv,
    local_sem,
    w_chain_send,
    w_chain_recv,
    w_group_send,
    w_group_recv,
    m_chain_send,
    m_chain_recv,
    f_chain_send,
    f_chain_recv,
    relay_send,
    own_sem,
    y_send,
    y_recv,
    r_send,
    r_recv,
    p_send,
    p_recv,
    h_send,
    h_recv,
):
    me = lax.axis_index("fsdp")
    core = me % CORES
    y = (me // CORES) % YS
    z = me // (CORES * YS)
    place = z % PLACES
    run = z // PLACES
    other = 1 - core
    octet = y * CORES + core

    def device(zz, yy, cc):
        return (zz * YS + yy) * CORES + cc

    def remote(src, dst, ssem, rsem, target):
        return pltpu.make_async_remote_copy(
            src_ref=src,
            dst_ref=dst,
            send_sem=ssem,
            recv_sem=rsem,
            device_id={"fsdp": target},
            device_id_type=MESH,
        )

    def when(cond, do):
        if cond is True:
            do()
        else:
            pl.when(cond)(do)

    def both(a, b):
        if a is True:
            return b
        if b is True:
            return a
        return jnp.logical_and(a, b)

    pending = []

    def send(cond, make):
        when(cond, lambda: make().start())
        pending.append((cond, make))

    def settle(batch):
        for cond, make in batch:
            when(cond, lambda make=make: make().wait_send())

    own_w = wbuf.at[run, place, core]
    w_copy = pltpu.make_async_copy(weight_hbm, own_w, local_sem.at[0])
    pool_copy = pltpu.make_async_copy(cache_hbm, pool, local_sem.at[1])
    new_copy = pltpu.make_async_copy(new_hidden_hbm, raw, local_sem.at[2])
    train_copy = pltpu.make_async_copy(
        train_hidden_hbm, hbuf.at[pl.ds(NEW, TRAIN_DEV)], local_sem.at[3]
    )
    small_copies = [
        pltpu.make_async_copy(src, dst, local_sem.at[4 + i])
        for i, (src, dst) in enumerate(
            (
                (destination_hbm, destination_ref),
                (queries_hbm, queries_ref),
                (table_hbm, table_ref),
                (length_hbm, length_ref),
                (documents_hbm, documents_ref),
                (bias_hbm, bias_ref),
                (train_queries_hbm, train_queries_ref),
            )
        )
    ]
    barrier = pltpu.get_barrier_semaphore()
    here = place * (YS * CORES) + octet
    for step in range(1, NEAR):
        pl.semaphore_signal(
            barrier,
            inc=1,
            device_id={"fsdp": run * NEAR + (here + step) % NEAR},
            device_id_type=MESH,
        )
    for step in range(1, RUNS):
        pl.semaphore_signal(
            barrier,
            inc=1,
            device_id={"fsdp": ((run + step) % RUNS) * NEAR + here},
            device_id_type=MESH,
        )
    expected = NEAR + RUNS - 2
    w_copy.start()
    new_copy.start()
    for copy in small_copies:
        copy.start()
    train_copy.start()
    pool_copy.start()
    small_copies[0].wait()
    lane = lax.broadcasted_iota(jnp.int32, (1, 128), 1)
    wanted = jnp.zeros((1, 128), jnp.float32)
    for r in range(ROWS_DEV):
        value = (destination_ref[r] + 1).astype(jnp.float32)
        hit = (lane // NEW == run) & ((lane % NEW) // 2 == r)
        wanted = jnp.where(hit, value, wanted)
    mbuf[run] = wanted

    small_copies[1].wait()
    for r in range(ROWS_DEV):
        both_tokens = queries_ref[r]
        qbuf[r] = jnp.concatenate(
            [both_tokens[:, g * HEAD_DIM : (g + 1) * HEAD_DIM] for g in range(GROUP)], axis=0
        )
    new_copy.wait()
    hbuf[0:NEW] = raw[...].reshape(NEW, WIDTH)
    pl.semaphore_wait(barrier, expected)

    class Along:
        def __init__(self, parts, relay=None):
            self.parts = parts
            self.relay = relay

        def start(self):
            for far in (1, 2, 3) if self.relay is not None else (3, 2, 1):
                for side in (1, -1):
                    target = run + side * far
                    cond = jnp.logical_and(target >= 0, target < RUNS)
                    for block, source, cs, cr, _, _ in self.parts:
                        src = block(run, place) if source is None else source
                        send(
                            cond,
                            lambda src=src, block=block, cs=cs, cr=cr, target=target: remote(
                                src,
                                block(run, place),
                                cs.at[target],
                                cr.at[run],
                                device(target * PLACES + place, y, core),
                            ),
                        )

        def chain(self, d):
            for cond, rr in quads(d):

                def do(rr=rr):
                    for block, _, cs, cr, _, _ in self.parts:
                        remote(
                            block(rr, place),
                            block(rr, place),
                            cs.at[rr],
                            cr.at[rr],
                            device(z, y, other),
                        ).wait_recv()

                when(cond, do)
                if d == 2 and self.relay is not None and RELAY_CHAIN:
                    onward = run + jnp.where(rr < run, 1, -1)
                    ahead = both(cond, jnp.logical_and(onward >= 0, onward < RUNS))
                    for i, (block, _, cs, cr, _, _) in enumerate(self.parts):
                        send(
                            ahead,
                            lambda rr=rr, i=i, block=block, cr=cr, onward=onward: remote(
                                block(rr, place),
                                block(rr, place),
                                self.relay.at[i, RUNS],
                                cr.at[rr],
                                device(onward * PLACES + place, y, core),
                            ),
                        )

        def spread(self, d):
            for cond, rr in quads(d):
                for far in (2, 1) if self.relay is not None and RELAY_GROUP else (3, 2, 1):
                    for side in (1, -1):
                        target = place + side * far
                        inside = both(cond, jnp.logical_and(target >= 0, target < PLACES))
                        for block, source, _, _, gs, gr in self.parts[:1]:
                            src = source if (d == 0 and source is not None) else block(rr, place)
                            send(
                                inside,
                                lambda src=src, block=block, gs=gs, gr=gr, rr=rr, target=target: (
                                    remote(
                                        src,
                                        block(rr, place),
                                        gs.at[rr, target],
                                        gr.at[rr, place],
                                        device(run * PLACES + target, y, core),
                                    )
                                ),
                            )

        def gather(self, d):
            for far in (2, 1, 3):
                for side in (1, -1):
                    pp = place + side * far
                    for cond, rr in quads(d):
                        inside = both(cond, jnp.logical_and(pp >= 0, pp < PLACES))

                        def do(rr=rr, pp=pp):
                            for block, _, _, _, gs, gr in self.parts[:1]:
                                remote(
                                    block(rr, pp),
                                    block(rr, pp),
                                    gs.at[rr, pp],
                                    gr.at[rr, pp],
                                    device(z, y, other),
                                ).wait_recv()

                        when(inside, do)
                        if far == 2 and self.relay is not None and RELAY_GROUP:
                            onward = place - side
                            ahead = both(
                                inside, jnp.logical_and(onward >= 0, onward < PLACES)
                            )
                            for i, (block, _, _, _, _, gr) in enumerate(self.parts[:1]):
                                send(
                                    ahead,
                                    lambda rr=rr, pp=pp, i=i, block=block, gr=gr, onward=onward: (
                                        remote(
                                            block(rr, pp),
                                            block(rr, pp),
                                            self.relay.at[i, rr],
                                            gr.at[rr, pp],
                                            device(run * PLACES + onward, y, core),
                                        )
                                    ),
                                )

    def quads(d):
        if d == 0:
            return [(True, run)]
        return [(run - d >= 0, run - d), (run + d < RUNS, run + d)]

    weights = Along(
        [
            (
                lambda rr, pp: wbuf.at[rr, pp, core],
                weight_hbm,
                w_chain_send,
                w_chain_recv,
                w_group_send,
                w_group_recv,
            ),
            (
                lambda rr, pp: mbuf.at[rr],
                None,
                m_chain_send,
                m_chain_recv,
                None,
                None,
            ),
        ],
        relay_send,
    )

    def pass_over(cond, rr):
        send(
            cond,
            lambda: remote(
                wbuf.at[rr, :, core],
                wbuf.at[rr, :, core],
                p_send.at[rr],
                p_recv.at[rr],
                device(z, y, other),
            ),
        )

    def chained(d):
        weights.chain(d)
        weights.spread(d)

    def gathered(d):
        weights.gather(d)
        for cond, rr in quads(d):
            pass_over(cond, rr)

    def columns(rr, pp, yy):
        start = ((rr * PLACES + pp) * YS + yy) * LANES
        return hbuf.at[:, pl.ds(pl.multiple_of(start, LANES), LANES)]

    def hidden_slot(rr, pp, yy):
        return gbuf.at[rr, yy, :, pl.ds(pp * LANES, LANES)]

    def own_copy(rr, pp):
        return pltpu.make_async_copy(
            columns(rr, pp, y), hidden_slot(rr, pp, y), own_sem.at[rr, pp]
        )

    def hidden_out():
        for rr in range(RUNS):
            for turn in (2, 1, 3):
                yy = (y + turn) % YS
                for pp in range(PLACES):
                    send(
                        True,
                        lambda rr=rr, pp=pp, turn=turn, yy=yy: remote(
                            columns(rr, pp, yy),
                            hidden_slot(rr, pp, y),
                            y_send.at[turn, rr, pp],
                            y_recv.at[y, rr, pp],
                            device(z, yy, core),
                        ),
                    )
            for pp in range(PLACES):
                own_copy(rr, pp).start()

    def hidden_in():
        for rr in range(RUNS):
            for pp in range(PLACES):
                own_copy(rr, pp).wait()
                for turn in (1, 3, 2):
                    yy = (y + turn) % YS
                    landed = hidden_slot(rr, pp, yy)
                    remote(
                        landed,
                        landed,
                        y_send.at[turn, rr, pp],
                        y_recv.at[yy, rr, pp],
                        device(z, y, other),
                    ).wait_recv()

    def multiply(rr):
        landed = wbuf.at[rr, :, other]
        remote(landed, landed, p_send.at[rr], p_recv.at[rr], device(z, y, other)).wait_recv()
        left = gbuf[rr].reshape(YS * ALL_ROWS, PLACES * LANES)
        right = wbuf[rr].reshape(PLACES * LANES, COLS)
        product = jnp.dot(left, right, preferred_element_type=jnp.float32)
        acc[...] += product.reshape(YS, ALL_ROWS, COLS)

    def multiplied(d):
        for cond, rr in quads(d):
            when(cond, lambda rr=rr: multiply(rr))

    def share_rows(part):
        return pl.ds(0, NEW) if part == 0 else pl.ds(NEW, TRAIN_DEV)

    def shares_out(part):
        for turn in (2, 1, 3):
            yy = (y + turn) % YS
            send(
                True,
                lambda turn=turn, yy=yy: remote(
                    acc.at[yy, share_rows(part)],
                    rbuf.at[y, share_rows(part)],
                    r_send.at[part, turn],
                    r_recv.at[part, y],
                    device(z, yy, core),
                ),
            )

    def shares_in(part):
        total = acc[y, share_rows(part)] + bias_ref[...]
        for turn in (1, 3, 2):
            yy = (y + turn) % YS
            landed = rbuf.at[yy, share_rows(part)]
            remote(
                landed, landed, r_send.at[part, turn], r_recv.at[part, yy], device(z, y, other)
            ).wait_recv()
            total = total + rbuf[yy, share_rows(part)]
        return total.astype(jnp.bfloat16)

    position = lax.broadcasted_iota(jnp.int32, (1, CONTEXT), 1)

    def old_scores(rows):
        for r in rows:
            keys = jnp.concatenate(
                [pool[table_ref[p, r], :, 0:HEAD_DIM] for p in range(MAX_PAGES)], axis=0
            )
            values = dot_nt(qbuf[r], keys) * SCALE
            scores[r] = jnp.where(position < length_ref[r], values, MASKED)

    acc[...] = jnp.zeros_like(acc)
    weights.start()
    weights.spread(0)
    train_copy.wait()
    hidden_out()
    pool_copy.wait()
    for copy in small_copies[2:]:
        copy.wait()
    old_scores(range(0, 16))
    w_copy.wait()
    chained(1)
    chained(2)
    gathered(0)
    chained(3)
    gathered(1)
    gathered(2)
    hidden_in()
    multiplied(0)
    multiplied(1)
    multiplied(2)
    gathered(3)
    multiplied(3)
    shares_out(0)
    fresh = shares_in(0)
    fbuf[run] = fresh
    kvbuf[0:NEW] = fresh

    rows_z = Along(
        [
            (
                lambda rr, pp: fbuf.at[rr],
                None,
                f_chain_send,
                f_chain_recv,
                None,
                None,
            )
        ]
    )

    new_column = lax.broadcasted_iota(jnp.int32, (CORES * GROUP, NEW), 1)
    new_token = lax.broadcasted_iota(jnp.int32, (CORES * GROUP, NEW), 0) % 2

    def decode(rows):
        for r in rows:
            values = jnp.concatenate(
                [pool[table_ref[p, r], :, HEAD_DIM : 2 * HEAD_DIM] for p in range(MAX_PAGES)],
                axis=0,
            )
            old = scores[r]
            new = dot_nt(qbuf[r], kvbuf[0:NEW, 0:HEAD_DIM]) * SCALE
            allowed = (new_column // 2 == r) & (new_column % 2 <= new_token)
            new = jnp.where(allowed, new, MASKED)
            highest = jnp.maximum(
                jnp.max(old, axis=1, keepdims=True), jnp.max(new, axis=1, keepdims=True)
            )
            old = jnp.exp(old - highest)
            new = jnp.exp(new - highest)
            total = jnp.sum(old, axis=1, keepdims=True) + jnp.sum(new, axis=1, keepdims=True)
            inverse = 1.0 / total
            result = jnp.dot(
                (old * inverse).astype(jnp.bfloat16), values, preferred_element_type=jnp.float32
            )
            result = result + jnp.dot(
                (new * inverse).astype(jnp.bfloat16),
                kvbuf[0:NEW, HEAD_DIM : 2 * HEAD_DIM],
                preferred_element_type=jnp.float32,
            )
            decoded_ref[r] = jnp.concatenate(
                [result[2 * g : 2 * g + 2] for g in range(GROUP)], axis=1
            ).astype(jnp.bfloat16)

    doc_row = jnp.broadcast_to(documents_ref[...], (TRAIN_DEV, TRAIN_DEV))
    row_id = lax.broadcasted_iota(jnp.int32, (TRAIN_DEV, TRAIN_DEV), 0)
    col_id = lax.broadcasted_iota(jnp.int32, (TRAIN_DEV, TRAIN_DEV), 1)
    doc_col = jnp.sum(jnp.where(row_id == col_id, doc_row, 0), axis=1, keepdims=True)
    train_mask = (col_id <= row_id) & (doc_row == doc_col)

    def train(heads):
        for g in heads:
            span = slice(g * HEAD_DIM, (g + 1) * HEAD_DIM)
            values = dot_nt(train_queries_ref[:, span], kvbuf[NEW:, 0:HEAD_DIM]) * SCALE
            values = jnp.where(train_mask, values, MASKED)
            expo = jnp.exp(values - jnp.max(values, axis=1, keepdims=True))
            inverse = 1.0 / jnp.sum(expo, axis=1, keepdims=True)
            result = jnp.dot(
                (expo * inverse).astype(jnp.bfloat16),
                kvbuf[NEW:, HEAD_DIM : 2 * HEAD_DIM],
                preferred_element_type=jnp.float32,
            )
            train_out_ref[:, span] = result.astype(jnp.bfloat16)

    weight_sends = list(pending)
    pending.clear()
    rows_z.start()
    shares_out(1)
    decode(range(0, 16))
    kvbuf[NEW:] = shares_in(1)
    train(range(0, 8))
    settle(weight_sends)
    out_row = lax.broadcasted_iota(jnp.int32, (NEAR * RUNS * 2, RUNS * NEW), 0)
    in_row = lax.broadcasted_iota(jnp.int32, (NEAR * RUNS * 2, RUNS * NEW), 1)
    owner = (run * NEAR + out_row // (RUNS * 2) + 1).astype(jnp.float32)
    same = ((out_row // 2) % RUNS == in_row // NEW) & (out_row % 2 == in_row % 2)
    asked = mbuf[0] + mbuf[1] + mbuf[2] + mbuf[3]
    chosen = jnp.where(same & (asked == owner), 1.0, 0.0).astype(jnp.bfloat16)
    rows_z.chain(1)
    rows_z.chain(2)
    rows_z.chain(3)
    rows = jnp.dot(
        chosen, fbuf[...].reshape(RUNS * NEW, COLS), preferred_element_type=jnp.float32
    )
    hstage[...] = rows.astype(jnp.bfloat16).reshape(NEAR, RUNS, 2, COLS)
    for step in range(NEAR - 1, 0, -1):
        target = (here + step) % NEAR
        send(
            True,
            lambda step=step, target=target: remote(
                hstage.at[target],
                hrecv.at[:, here],
                h_send.at[step],
                h_recv.at[here],
                run * NEAR + target,
            ),
        )
    hrecv[:, here] = hstage[here]
    for step in range(1, NEAR):
        source = (here + step) % NEAR
        remote(
            hstage.at[source],
            hrecv.at[:, source],
            h_send.at[step],
            h_recv.at[source],
            run * NEAR + source,
        ).wait_recv()
    handover_ref[...] = hrecv[...]
    settle(pending)


def finish(decoded, attended, handed, decoded_out, attended_out, handed_out):
    decoded_out[...] = decoded[...]
    attended_out[...] = attended[...]
    handed_out[...] = handed[...]


def local(
    new_hidden,
    new_queries,
    paged_cache,
    block_table,
    lengths,
    destination,
    train_hidden,
    train_queries,
    documents,
    project_weight,
    project_bias,
):
    vmem = pl.BlockSpec(memory_space=pltpu.VMEM)
    hbm = pl.BlockSpec(memory_space=pltpu.HBM)
    dma = pltpu.SemaphoreType.DMA
    along = [dma((RUNS,)), dma((RUNS,)), dma((RUNS, PLACES)), dma((RUNS, PLACES))]
    decoded, attended, handed = pl.pallas_call(
        kernel,
        out_shape=(
            jax.ShapeDtypeStruct((ROWS_DEV, 2, GROUP * HEAD_DIM), jnp.bfloat16),
            jax.ShapeDtypeStruct((TRAIN_DEV, GROUP * HEAD_DIM), jnp.bfloat16),
            jax.ShapeDtypeStruct((RUNS, NEAR, 2, COLS), jnp.bfloat16),
        ),
        in_specs=[hbm] * 11,
        out_specs=(vmem, vmem, vmem),
        scratch_shapes=[
            pltpu.SMEM((MAX_PAGES, ROWS_DEV), jnp.int32),
            pltpu.SMEM((ROWS_DEV,), jnp.int32),
            pltpu.SMEM((ROWS_DEV,), jnp.int32),
            pltpu.VMEM((1, TRAIN_DEV), jnp.int32),
            pltpu.VMEM((1, COLS), jnp.float32),
            pltpu.VMEM((ROWS_DEV, 2, GROUP * HEAD_DIM), jnp.bfloat16),
            pltpu.VMEM((TRAIN_DEV, GROUP * HEAD_DIM), jnp.bfloat16),
            pltpu.VMEM((RUNS, PLACES, CORES, BLOCK, COLS), jnp.bfloat16),
            pltpu.VMEM((ALL_ROWS, WIDTH), jnp.bfloat16),
            pltpu.VMEM((ROWS_DEV, 2, WIDTH), jnp.bfloat16),
            pltpu.VMEM((ROWS_DEV, 2 * GROUP, HEAD_DIM), jnp.bfloat16),
            pltpu.VMEM((paged_cache.shape[0], PAGE, COLS), jnp.bfloat16),
            pltpu.VMEM((RUNS, 1, 128), jnp.float32),
            pltpu.VMEM((RUNS, NEW, COLS), jnp.bfloat16),
            pltpu.VMEM((RUNS, YS, ALL_ROWS, PLACES * LANES), jnp.bfloat16),
            pltpu.VMEM((YS, ALL_ROWS, COLS), jnp.float32),
            pltpu.VMEM((YS, ALL_ROWS, COLS), jnp.float32),
            pltpu.VMEM((ALL_ROWS, COLS), jnp.bfloat16),
            pltpu.VMEM((ROWS_DEV, CORES * GROUP, CONTEXT), jnp.float32),
            pltpu.VMEM((NEAR, RUNS, 2, COLS), jnp.bfloat16),
            pltpu.VMEM((RUNS, NEAR, 2, COLS), jnp.bfloat16),
            dma((11,)),
            *along,
            dma((RUNS,)),
            dma((RUNS,)),
            dma((RUNS,)),
            dma((RUNS,)),
            dma((2, RUNS + 1)),
            dma((RUNS, PLACES)),
            dma((YS, RUNS, PLACES)),
            dma((YS, RUNS, PLACES)),
            dma((2, YS)),
            dma((2, YS)),
            dma((RUNS,)),
            dma((RUNS,)),
            dma((NEAR,)),
            dma((NEAR,)),
        ],
        compiler_params=pltpu.CompilerParams(
            collective_id=0, has_side_effects=True, vmem_limit_bytes=24 * 1024 * 1024
        ),
    )(
        *(
            pltpu.with_memory_space_constraint(x, pltpu.HBM)
            for x in (
                block_table.T,
                lengths,
                destination,
                documents,
                project_bias.reshape(1, COLS),
                new_queries,
                train_queries,
                new_hidden,
                train_hidden,
                paged_cache,
                project_weight,
            )
        )
    )
    handed = handed.reshape(RUNS * PLACES * YS * CORES, 2, COLS)
    return pl.pallas_call(
        finish,
        out_shape=tuple(
            jax.ShapeDtypeStruct(x.shape, x.dtype) for x in (decoded, attended, handed)
        ),
        in_specs=[vmem] * 3,
        out_specs=(vmem,) * 3,
        compiler_params=pltpu.CompilerParams(vmem_limit_bytes=4 * 1024 * 1024),
    )(decoded, attended, handed)


def solution(mesh):
    return jax.shard_map(
        local,
        mesh=mesh,
        in_specs=(
            P("fsdp", None, None),
            P("fsdp", None, "tensor"),
            P("fsdp", None, "tensor"),
            P("fsdp", None),
            P("fsdp"),
            P("fsdp"),
            P("fsdp", None),
            P("fsdp", "tensor"),
            P("fsdp", None),
            P("fsdp", "tensor"),
            P("tensor"),
        ),
        out_specs=(P("fsdp", None, "tensor"), P("fsdp", "tensor"), P("fsdp", None, "tensor")),
        check_vma=False,
    )
```
